256 devices in a mesh: ty: 16 (over y, z_lo), tx: 16 (over z_hi, x, core).
Axes of the slice: x: 4, y: 4, z: 8 (z_hi: 2, z_lo: 4; z = z_hi * 4 + z_lo), core: 2. Of those that a mesh axis runs over, the one named last changes fastest.
Arguments:
- object_field: float32 [3, 2, 2048, 2048], P(None, None, 'ty', 'tx'), may hold values from -6 to 6
- probe: float32 [2, 256, 256], replicated, may hold values from -6 to 6
- propagator_phase: float32 [256, 256], replicated, may hold values from -3.140625 to 3.140625
- patterns: float32 [16, 16, 1, 256, 256], P('ty', 'tx'), may hold values from 0 to 2
- scan_positions: int32 [16, 16, 1, 2], P('ty', 'tx'), may hold values from 0 to 255
Outputs:
- updated_object: float32 [3, 2, 2048, 2048], P(None, None, 'ty', 'tx')
The draws below stay inside these ranges and needn't reach their ends.
All inputs are finite; a program needn't handle non-finite values.
Results may differ from the reference program's by a relative error of at most 0.0003.
Values sent between devices are 32-bit elements; how exact they have to be, the bound alone decides.
No kernel may reach another device: no remote copies, remote signals or barrier semaphores. Data moves between devices by JAX's collectives and lax.ppermute only.
A program may use at most 64 MiB of HBM per device.

```python
import jax
import jax.numpy as jnp
from jax import lax

TILE = 256
MARGIN = 64
SLICES = 3
STEPS = 2
PAT = 1
TILES_Y = 16
TILES_X = 16
NY = 2048
NX = 2048


def touch_ends(drawn, own_key, least, largest):
    longest = drawn.shape.index(max(drawn.shape))
    spots = []
    for shift in (0, 1):
        where = [jax.random.randint(jax.random.fold_in(own_key, axis), (), 0, length) for axis, length in enumerate(drawn.shape)]
        where[longest] = (where[longest] + shift) % drawn.shape[longest]
        spots.append(tuple(where))
    return drawn.at[spots[0]].set(least).at[spots[1]].set(largest)


def shard_levels(stream_key, shape, pieces, low, high):
    def one(position, blocks):
        heights = jax.random.uniform(jax.random.fold_in(jax.random.fold_in(stream_key, 6), position), (blocks,), jnp.float32, low / len(pieces), high / len(pieces))
        return jnp.repeat(jnp.exp(heights), shape[position] // blocks).reshape((-1,) + (1,) * (len(shape) - position - 1))

    factor_of = one(*pieces[0])
    for cut in pieces[1:]:
        factor_of = factor_of * one(*cut)
    return factor_of


def gaussian(key, shape, spread, bound, cuts=(), kind=jnp.bfloat16):
    factor_of = shard_levels(key, shape, cuts, -0.22, 0.18) if cuts else 1.0
    array = jax.random.normal(key, shape, jnp.float32) * spread * factor_of
    return jnp.minimum(jnp.maximum(array, -bound), bound).astype(kind)


def setup_inputs(seed: int = 0) -> dict:
    arg_keys = jax.random.split(jax.random.key(seed), 6)
    object_field = gaussian(arg_keys[0], (SLICES, 2, NY, NX), 0.7, 6.0, ((2, 16), (3, 16)), jnp.float32)
    probe = gaussian(arg_keys[1], (2, TILE, TILE), 0.7, 6.0, (), jnp.float32)
    propagator_phase = jnp.clip(jax.random.uniform(arg_keys[2], (TILE, TILE), jnp.float32, -3.140625, 3.140625), -3.140625, 3.140625)
    patterns = jnp.clip(2.0 * jax.random.uniform(arg_keys[3], (TILES_Y, TILES_X, PAT, TILE, TILE), jnp.float32) ** shard_levels(arg_keys[3], (TILES_Y, TILES_X, PAT, TILE, TILE), ((0, 16), (1, 16)), -0.2, 0.2), 0.0, 2.0)
    scan_positions = touch_ends(jax.random.randint(arg_keys[4], (TILES_Y, TILES_X, PAT, 2), 0, TILE), jax.random.fold_in(arg_keys[4], 1), 0, TILE - 1).astype(jnp.int32)
    return {"object_field": object_field, "probe": probe, "propagator_phase": propagator_phase, "patterns": patterns, "scan_positions": scan_positions}


step_size = 0.05


def forward_dft(field):
    return jnp.fft.fft2(field, axes=(-2, -1), norm="ortho")


def inverse_dft(field):
    return jnp.fft.ifft2(field, axes=(-2, -1), norm="ortho")


def tile_gradient(tile, tile_patterns, positions, probe, kernel):
    slices = [lax.complex(tile[layer, 0], tile[layer, 1]) for layer in range(SLICES)]
    gradients = [jnp.zeros_like(slices[0]) for layer in range(SLICES)]
    for pattern_index in range(PAT):
        shift_rows = positions[pattern_index, 0]
        shift_cols = positions[pattern_index, 1]
        probe_real = jnp.roll(probe[0], (shift_rows, shift_cols), axis=(0, 1))
        probe_imag = jnp.roll(probe[1], (shift_rows, shift_cols), axis=(0, 1))
        lit = lax.complex(probe_real, probe_imag)
        wave = lit * slices[0]
        entering = []
        for layer in range(1, SLICES):
            moved = inverse_dft(kernel * forward_dft(wave))
            entering.append(moved)
            wave = moved * slices[layer]
        far_field = forward_dft(wave)
        power = jnp.real(far_field) ** 2 + jnp.imag(far_field) ** 2
        upstream = inverse_dft((power - tile_patterns[pattern_index]) * far_field)
        for layer in range(SLICES - 1, 0, -1):
            gradients[layer] = gradients[layer] + jnp.conj(entering[layer - 1]) * upstream
            upstream = inverse_dft(jnp.conj(kernel) * forward_dft(jnp.conj(slices[layer]) * upstream))
        gradients[0] = gradients[0] + jnp.conj(lit) * upstream
    return jnp.stack([jnp.stack([jnp.real(grad), jnp.imag(grad)]) for grad in gradients])


def shift_tiles(grid, offset, axis):
    zeros = jnp.zeros_like(lax.slice_in_dim(grid, 0, 1, axis=axis))
    if offset == 1:
        return jnp.concatenate([zeros, lax.slice_in_dim(grid, 0, grid.shape[axis] - 1, axis=axis)], axis=axis)
    return jnp.concatenate([lax.slice_in_dim(grid, 1, grid.shape[axis], axis=axis), zeros], axis=axis)


def owner_sum(grid, tile_axis, pixel_axis):
    core = TILE - 2 * MARGIN
    middle = lax.slice_in_dim(grid, MARGIN, MARGIN + core, axis=pixel_axis)
    from_above = lax.slice_in_dim(shift_tiles(grid, 1, tile_axis), TILE - MARGIN, TILE, axis=pixel_axis)
    from_below = lax.slice_in_dim(shift_tiles(grid, -1, tile_axis), 0, MARGIN, axis=pixel_axis)
    widths_above = [(0, 0)] * grid.ndim
    widths_above[pixel_axis] = (0, core - MARGIN)
    widths_below = [(0, 0)] * grid.ndim
    widths_below[pixel_axis] = (core - MARGIN, 0)
    return middle + jnp.pad(from_above, widths_above) + jnp.pad(from_below, widths_below)


def reference(object_field, probe, propagator_phase, patterns, scan_positions):
    kernel = lax.complex(jnp.cos(propagator_phase), jnp.sin(propagator_phase))
    core = TILE - 2 * MARGIN
    current = object_field
    for iteration in range(STEPS):
        padded = jnp.pad(current, ((0, 0), (0, 0), (MARGIN, MARGIN), (MARGIN, MARGIN)))

        def one_tile(flat_index):
            tile_row = flat_index // TILES_X
            tile_col = flat_index % TILES_X
            zero = jnp.zeros((), jnp.int32)
            tile = lax.dynamic_slice(padded, (zero, zero, (tile_row * core).astype(jnp.int32), (tile_col * core).astype(jnp.int32)), (SLICES, 2, TILE, TILE))
            return tile_gradient(tile, patterns[tile_row, tile_col], scan_positions[tile_row, tile_col], probe, kernel)

        grads = lax.map(one_tile, jnp.arange(TILES_Y * TILES_X, dtype=jnp.int32))
        grads = grads.reshape(TILES_Y, TILES_X, SLICES, 2, TILE, TILE)
        summed = owner_sum(grads, 0, 4)
        summed = owner_sum(summed, 1, 5)
        summed = jnp.transpose(summed, (2, 3, 0, 4, 1, 5)).reshape(SLICES, 2, TILES_Y * core, TILES_X * core)
        current = current - step_size * summed
    return current
```

```python
import functools
import math

import jax
import jax.numpy as jnp
import numpy as np
from jax import lax
from jax.experimental import pallas as pl
from jax.experimental.pallas import tpu as pltpu
from jax.sharding import PartitionSpec as P

MARGIN = 64
CORE = 128
TILE = 256
SLICES = 3
STEPS = 2
STEP_SIZE = 0.05


def half_tables():
    index = np.arange(CORE)
    tables = []
    for parity in range(2):
        freq = 2 * index + parity
        angle = 2.0 * math.pi * ((freq[:, None] * index[None, :]) % TILE) / TILE
        real, imag = np.cos(angle) / 16.0, -np.sin(angle) / 16.0
        block = np.block([[real, -imag], [imag, real]]).astype(np.float32)
        for table in (block, block.T):
            high = table.astype(jnp.bfloat16)
            low = (table - high.astype(np.float32)).astype(jnp.bfloat16)
            tables.append(np.stack([high, low]))
    return np.stack(tables)


def order_table():
    table = np.zeros((TILE, TILE), np.float32)
    index = np.arange(CORE)
    table[index, 2 * index] = 1.0
    table[CORE + index, 2 * index + 1] = 1.0
    return np.stack([table, table.T]).astype(jnp.bfloat16)


def dot(left, right):
    return jnp.dot(left, right, preferred_element_type=jnp.float32)


def split(value):
    high = value.astype(jnp.bfloat16)
    low = (value - high.astype(jnp.float32)).astype(jnp.bfloat16)
    return high, low


def from_left(tables, which, value):
    high, low = split(value)
    t_high, t_low = tables[which, 0], tables[which, 1]
    return dot(t_high, high) + (dot(t_high, low) + dot(t_low, high))


def from_right(tables, which, value):
    high, low = split(value)
    t_high, t_low = tables[which, 0], tables[which, 1]
    return dot(high, t_high) + (dot(high, t_low) + dot(low, t_high))


def stack(*rows):
    return jnp.concatenate(rows, axis=0)


def beside(*cols):
    return jnp.concatenate(cols, axis=1)


def forward(tables, real, imag):
    half = []
    for parity in range(2):
        if parity == 0:
            mixed = stack(real[:CORE] + real[CORE:], imag[:CORE] + imag[CORE:])
        else:
            mixed = stack(real[:CORE] - real[CORE:], imag[:CORE] - imag[CORE:])
        half.append(from_left(tables, 2 * parity, mixed))
    out = []
    for parity in range(2):
        rows = []
        for value in half:
            parts = []
            for part in (value[:CORE], value[CORE:]):
                first, second = part[:, :CORE], part[:, CORE:]
                parts.append(first + second if parity == 0 else first - second)
            rows.append(beside(*parts))
        out.append(from_right(tables, 2 * parity + 1, stack(*rows)))
    return out


def backward(tables, freq):
    even = from_right(tables, 0, freq[0])
    odd = from_right(tables, 2, freq[1])
    first, second = even + odd, even - odd
    half = []
    for parity in range(2):
        rows = slice(parity * CORE, (parity + 1) * CORE)
        mixed = stack(
            beside(first[rows, :CORE], second[rows, :CORE]),
            beside(first[rows, CORE:], second[rows, CORE:]),
        )
        half.append(from_left(tables, 2 * parity + 1, mixed))
    even, odd = half
    real = stack(even[:CORE] + odd[:CORE], even[:CORE] - odd[:CORE])
    imag = stack(even[CORE:] + odd[CORE:], even[CORE:] - odd[CORE:])
    return real, imag


def propagate(tables, real, imag, wave, sign):
    freq = forward(tables, real, imag)
    out = []
    for parity in range(2):
        real, imag = freq[parity][:, :CORE], freq[parity][:, CORE:]
        cols = pl.ds(parity * CORE, CORE)
        h_real, h_imag = wave[0, :, cols], wave[1, :, cols]
        if sign < 0:
            out.append(beside(real * h_real + imag * h_imag, imag * h_real - real * h_imag))
        else:
            out.append(beside(real * h_real - imag * h_imag, imag * h_real + real * h_imag))
    return backward(tables, out)


def low_lanes(shape):
    return lax.broadcasted_iota(jnp.int32, shape, len(shape) - 1) < MARGIN


def turned(value):
    return pltpu.roll(value, MARGIN, 1)


def step_kernel(
    par, mid, near, far, lit, wave, patterns, tables, part, send_near, send_far, tile, field, up
):
    even = par[1] == 0
    low = low_lanes((TILE, CORE)) == even
    for layer in range(SLICES):
        e, o = near[layer], far[layer]
        tile[layer, 0, :, :CORE] = mid[layer, 0]
        tile[layer, 1, :, :CORE] = mid[layer, 1]
        tile[layer, 0, :, CORE:] = jnp.where(low, e, o)
        tile[layer, 1, :, CORE:] = turned(jnp.where(low, o, e))
    field[0, 0] = lit[0]
    field[0, 1] = lit[1]

    def ahead(layer, carry):
        f_real, f_imag = field[layer, 0], field[layer, 1]
        t_real, t_imag = tile[layer, 0], tile[layer, 1]
        real, imag = propagate(
            tables, f_real * t_real - f_imag * t_imag, f_real * t_imag + f_imag * t_real, wave, 1
        )
        field[layer + 1, 0] = real
        field[layer + 1, 1] = imag
        return carry

    lax.fori_loop(0, SLICES - 1, ahead, 0)
    f_real, f_imag = field[SLICES - 1, 0], field[SLICES - 1, 1]
    t_real, t_imag = tile[SLICES - 1, 0], tile[SLICES - 1, 1]
    freq = forward(tables, f_real * t_real - f_imag * t_imag, f_real * t_imag + f_imag * t_real)
    out = []
    for parity in range(2):
        real, imag = freq[parity][:, :CORE], freq[parity][:, CORE:]
        residue = real * real + imag * imag - patterns[:, pl.ds(parity * CORE, CORE)]
        out.append(beside(residue * real, residue * imag))
    real, imag = backward(tables, out)
    up[0] = real
    up[1] = imag

    def gradient(layer):
        f_real, f_imag = field[layer, 0], field[layer, 1]
        u_real, u_imag = up[0], up[1]
        real = f_real * u_real + f_imag * u_imag
        imag = f_real * u_imag - f_imag * u_real
        part[layer, 0] = real[:, :CORE]
        part[layer, 1] = imag[:, :CORE]
        straight, other = real[:, CORE:], turned(imag[:, CORE:])
        send_near[layer] = jnp.where(low, straight, other)
        send_far[layer] = jnp.where(low, other, straight)

    def behind(turn, carry):
        layer = SLICES - 1 - turn
        gradient(layer)
        t_real, t_imag = tile[layer, 0], tile[layer, 1]
        u_real, u_imag = up[0], up[1]
        real, imag = propagate(
            tables, t_real * u_real + t_imag * u_imag, t_real * u_imag - t_imag * u_real, wave, -1
        )
        up[0] = real
        up[1] = imag
        return carry

    lax.fori_loop(0, SLICES - 1, behind, 0)
    gradient(0)


def call(body, outs, scratch=(), smem=1, count=0):
    return pl.pallas_call(
        body,
        out_shape=[jax.ShapeDtypeStruct(shape, jnp.float32) for shape in outs],
        in_specs=[pl.BlockSpec(memory_space=pltpu.SMEM)] * smem
        + [pl.BlockSpec(memory_space=pltpu.VMEM)] * count,
        out_specs=[pl.BlockSpec(memory_space=pltpu.VMEM)] * len(outs),
        scratch_shapes=list(scratch),
        name=body.__name__,
    )


PART = (SLICES, 2, TILE, CORE)
PACK = (SLICES, TILE, CORE)


def step(*args):
    return call(
        step_kernel,
        (PART, PACK, PACK),
        (
            pltpu.VMEM((SLICES, 2, TILE, TILE), jnp.float32),
            pltpu.VMEM((SLICES, 2, TILE, TILE), jnp.float32),
            pltpu.VMEM((2, TILE, TILE), jnp.float32),
        ),
        count=7,
    )(*args)


def three(value):
    high = value.astype(jnp.bfloat16)
    rest = value - high.astype(jnp.float32)
    middle = rest.astype(jnp.bfloat16)
    low = (rest - middle.astype(jnp.float32)).astype(jnp.bfloat16)
    return high, middle, low


def reorder(order, value):
    high, middle, low = three(value)
    rows = (dot(order[0], high) + dot(order[0], middle)) + dot(order[0], low)
    high, middle, low = three(rows)
    return (dot(high, order[1]) + dot(middle, order[1])) + dot(low, order[1])


def setup_kernel(positions, probe, phase, patterns, order, lit, ordered_phase, ordered_patterns):
    rows = lax.rem(positions[0] + (TILE - MARGIN), TILE)
    cols = lax.rem(positions[1] + (TILE - MARGIN), TILE)
    for part in range(2):
        lit[part] = pltpu.roll(pltpu.roll(probe[part], rows, 0), cols, 1)
    ordered_phase[...] = reorder(order, phase[...])
    ordered_patterns[...] = reorder(order, patterns[...])


def setup(positions, probe, phase, patterns, order):
    shapes = ((2, TILE, TILE), (TILE, TILE), (TILE, TILE))
    return call(setup_kernel, shapes, count=4)(positions, probe, phase, patterns, order)


def pack_columns(even, mid, send_near, send_far):
    low = low_lanes((TILE, CORE)) == even
    for layer in range(SLICES):
        straight, other = mid[layer, 0], turned(mid[layer, 1])
        send_near[layer] = jnp.where(low, other, straight)
        send_far[layer] = jnp.where(low, straight, other)


def assemble_kernel(par, core, near, far, mid, send_near, send_far):
    even = par[0] == 0
    for layer in range(SLICES):
        for part in range(2):
            e, o = near[layer, part], far[layer, part]
            mid[layer, part, :CORE] = core[layer, part]
            mid[layer, part, CORE : CORE + MARGIN] = jnp.where(even, e, o)
            mid[layer, part, CORE + MARGIN :] = jnp.where(even, o, e)
    pack_columns(par[1] == 0, mid, send_near, send_far)


def assemble(*args):
    return call(assemble_kernel, (PART, PACK, PACK), count=3)(*args)


def add_columns(even, part, near, far):
    low = low_lanes((TILE, CORE)) == even
    out = []
    for layer in range(SLICES):
        e, o = near[layer], far[layer]
        out.append(
            (
                part[layer, 0] + jnp.where(low, o, e),
                part[layer, 1] + turned(jnp.where(low, e, o)),
            )
        )
    return out


def share_kernel(par, part, near, far, total, send_near, send_far):
    even = par[0] == 0
    sums = add_columns(par[1] == 0, part, near, far)
    for layer in range(SLICES):
        for c in range(2):
            value = sums[layer][c]
            total[layer, c] = value
            a, b, d, e = (value[k * MARGIN : (k + 1) * MARGIN] for k in range(4))
            send_near[layer, c, :MARGIN] = jnp.where(even, b, e)
            send_near[layer, c, MARGIN:] = jnp.where(even, d, a)
            send_far[layer, c, :MARGIN] = jnp.where(even, e, b)
            send_far[layer, c, MARGIN:] = jnp.where(even, a, d)


def share(*args):
    half = (SLICES, 2, CORE, CORE)
    return call(share_kernel, (PART, half, half), count=3)(*args)


def update_kernel(par, mid, total, near, far, new, send_near, send_far):
    even = par[0] == 0
    above = jnp.where(par[2] == 0, 0.0, STEP_SIZE)
    below = jnp.where(par[3] == 0, 0.0, STEP_SIZE)
    for layer in range(SLICES):
        for c in range(2):
            e, o = near[layer, c], far[layer, c]
            down = jnp.where(even, e, o)
            up = jnp.where(even, o, e)
            for k, (added, scale) in enumerate(
                (
                    (up[MARGIN:], STEP_SIZE),
                    (down[:MARGIN], STEP_SIZE),
                    (down[MARGIN:], below),
                    (up[:MARGIN], above),
                )
            ):
                rows = pl.ds(k * MARGIN, MARGIN)
                new[layer, c, rows] = mid[layer, c, rows] - scale * (total[layer, c, rows] + added)
    pack_columns(par[1] == 0, new, send_near, send_far)


def update(*args):
    return call(update_kernel, (PART, PACK, PACK), count=4)(*args)


def close_kernel(par, part, near, far, total, send_near, send_far):
    even = par[0] == 0
    sums = add_columns(par[1] == 0, part, near, far)
    for layer in range(SLICES):
        for c in range(2):
            value = sums[layer][c]
            total[layer, c] = value[:CORE]
            below, above = value[CORE : CORE + MARGIN], value[CORE + MARGIN :]
            send_near[layer, c] = jnp.where(even, below, above)
            send_far[layer, c] = jnp.where(even, above, below)


def close(*args):
    rim = (SLICES, 2, MARGIN, CORE)
    return call(close_kernel, ((SLICES, 2, CORE, CORE), rim, rim), count=3)(*args)


def finish_kernel(par, mid, total, near, far, out):
    even = par[0] == 0
    for layer in range(SLICES):
        for c in range(2):
            e, o = near[layer, c], far[layer, c]
            for k, added in enumerate((jnp.where(even, o, e), jnp.where(even, e, o))):
                rows = pl.ds(k * MARGIN, MARGIN)
                out[layer, c, rows] = mid[layer, c, rows] - STEP_SIZE * (
                    total[layer, c, rows] + added
                )


def finish(*args):
    return call(finish_kernel, ((SLICES, 2, CORE, CORE),), count=4)(*args)[0]


def swap(axis, near, far):
    count = lax.axis_size(axis)

    def route(first):
        pairs = [(i, i + 1) for i in range(first, count - 1, 2)]
        return pairs + [(j, i) for i, j in pairs]

    far = lax.ppermute(far, axis, route(1))
    near = lax.ppermute(near, axis, route(0))
    return near, far


def shards(object_field, probe, propagator_phase, patterns, scan_positions):
    row, col = lax.axis_index("ty"), lax.axis_index("tx")
    par = jnp.stack([row % 2, col % 2, row, lax.axis_size("ty") - 1 - row]).astype(jnp.int32)
    even = row % 2 == 0
    top, bottom = object_field[:, :, :MARGIN], object_field[:, :, MARGIN:]
    near, far = swap("ty", jnp.where(even, bottom, top), jnp.where(even, top, bottom))
    lit, phase, ordered = setup(
        scan_positions[0, 0, 0], probe, propagator_phase, patterns[0, 0, 0], order_table()
    )
    wave = jnp.stack([jnp.cos(phase), jnp.sin(phase)])
    tables = jnp.asarray(half_tables())
    mid, near, far = assemble(par, object_field, near, far)
    for turn in range(STEPS):
        near, far = swap("tx", near, far)
        part, near, far = step(par, mid, near, far, lit, wave, ordered, tables)
        near, far = swap("tx", near, far)
        if turn < STEPS - 1:
            total, near, far = share(par, part, near, far)
            near, far = swap("ty", near, far)
            mid, near, far = update(par, mid, total, near, far)
    total, near, far = close(par, part, near, far)
    near, far = swap("ty", near, far)
    return finish(par, mid, total, near, far)


def solution(mesh):
    placed = (
        P(None, None, "ty", "tx"),
        P(),
        P(),
        P("ty", "tx", None, None, None),
        P("ty", "tx", None, None),
    )
    return jax.shard_map(
        shards, mesh=mesh, in_specs=placed, out_specs=P(None, None, "ty", "tx"), check_vma=False
    )
```

```python
import functools
import math

import jax
import jax.numpy as jnp
import numpy as np
from jax import lax
from jax.experimental import pallas as pl
from jax.experimental.pallas import tpu as pltpu
from jax.sharding import PartitionSpec as P

MARGIN = 64
CORE = 128
TILE = 256
SLICES = 3
STEPS = 2
STEP_SIZE = 0.05


def half_tables():
    index = np.arange(CORE)
    tables = []
    for parity in range(2):
        freq = 2 * index + parity
        angle = 2.0 * math.pi * ((freq[:, None] * index[None, :]) % TILE) / TILE
        real, imag = np.cos(angle) / 16.0, -np.sin(angle) / 16.0
        block = np.block([[real, -imag], [imag, real]]).astype(np.float32)
        for table in (block, block.T):
            high = table.astype(jnp.bfloat16)
            low = (table - high.astype(np.float32)).astype(jnp.bfloat16)
            tables.append(np.stack([high, low]))
    return np.stack(tables)


def order_table():
    table = np.zeros((TILE, TILE), np.float32)
    index = np.arange(CORE)
    table[index, 2 * index] = 1.0
    table[CORE + index, 2 * index + 1] = 1.0
    return np.stack([table, table.T]).astype(jnp.bfloat16)


def dot(left, right):
    return jnp.dot(left, right, preferred_element_type=jnp.float32)


def split(value):
    high = value.astype(jnp.bfloat16)
    low = (value - high.astype(jnp.float32)).astype(jnp.bfloat16)
    return high, low


def from_left(tables, which, value):
    high, low = split(value)
    t_high, t_low = tables[which, 0], tables[which, 1]
    return dot(t_high, high) + (dot(t_high, low) + dot(t_low, high))


def from_right(tables, which, value):
    high, low = split(value)
    t_high, t_low = tables[which, 0], tables[which, 1]
    return dot(high, t_high) + (dot(high, t_low) + dot(low, t_high))


def stack(*rows):
    return jnp.concatenate(rows, axis=0)


def beside(*cols):
    return jnp.concatenate(cols, axis=1)


def forward(tables, real, imag):
    half = []
    for parity in range(2):
        if parity == 0:
            mixed = stack(real[:CORE] + real[CORE:], imag[:CORE] + imag[CORE:])
        else:
            mixed = stack(real[:CORE] - real[CORE:], imag[:CORE] - imag[CORE:])
        half.append(from_left(tables, 2 * parity, mixed))
    out = []
    for parity in range(2):
        rows = []
        for value in half:
            parts = []
            for part in (value[:CORE], value[CORE:]):
                first, second = part[:, :CORE], part[:, CORE:]
                parts.append(first + second if parity == 0 else first - second)
            rows.append(beside(*parts))
        out.append(from_right(tables, 2 * parity + 1, stack(*rows)))
    return out


def backward(tables, freq):
    even = from_right(tables, 0, freq[0])
    odd = from_right(tables, 2, freq[1])
    first, second = even + odd, even - odd
    half = []
    for parity in range(2):
        rows = slice(parity * CORE, (parity + 1) * CORE)
        mixed = stack(
            beside(first[rows, :CORE], second[rows, :CORE]),
            beside(first[rows, CORE:], second[rows, CORE:]),
        )
        half.append(from_left(tables, 2 * parity + 1, mixed))
    even, odd = half
    real = stack(even[:CORE] + odd[:CORE], even[:CORE] - odd[:CORE])
    imag = stack(even[CORE:] + odd[CORE:], even[CORE:] - odd[CORE:])
    return real, imag


def propagate(tables, real, imag, wave, sign):
    freq = forward(tables, real, imag)
    out = []
    for parity in range(2):
        real, imag = freq[parity][:, :CORE], freq[parity][:, CORE:]
        cols = pl.ds(parity * CORE, CORE)
        h_real, h_imag = wave[0, :, cols], wave[1, :, cols]
        if sign < 0:
            out.append(beside(real * h_real + imag * h_imag, imag * h_real - real * h_imag))
        else:
            out.append(beside(real * h_real - imag * h_imag, imag * h_real + real * h_imag))
    return backward(tables, out)


def low_lanes(shape):
    return lax.broadcasted_iota(jnp.int32, shape, len(shape) - 1) < MARGIN


def turned(value):
    return pltpu.roll(value, MARGIN, 1)


def step_kernel(
    par, mid, near, far, lit, wave, patterns, tables, part, send_near, send_far, tile, field, up
):
    even = par[1] == 0
    low = low_lanes((TILE, CORE)) == even
    for layer in range(SLICES):
        e, o = near[layer], far[layer]
        tile[layer, 0, :, :CORE] = mid[layer, 0]
        tile[layer, 1, :, :CORE] = mid[layer, 1]
        tile[layer, 0, :, CORE:] = jnp.where(low, e, o)
        tile[layer, 1, :, CORE:] = turned(jnp.where(low, o, e))
    field[0, 0] = lit[0]
    field[0, 1] = lit[1]

    def ahead(layer, carry):
        f_real, f_imag = field[layer, 0], field[layer, 1]
        t_real, t_imag = tile[layer, 0], tile[layer, 1]
        real, imag = propagate(
            tables, f_real * t_real - f_imag * t_imag, f_real * t_imag + f_imag * t_real, wave, 1
        )
        field[layer + 1, 0] = real
        field[layer + 1, 1] = imag
        return carry

    lax.fori_loop(0, SLICES - 1, ahead, 0)
    f_real, f_imag = field[SLICES - 1, 0], field[SLICES - 1, 1]
    t_real, t_imag = tile[SLICES - 1, 0], tile[SLICES - 1, 1]
    freq = forward(tables, f_real * t_real - f_imag * t_imag, f_real * t_imag + f_imag * t_real)
    out = []
    for parity in range(2):
        real, imag = freq[parity][:, :CORE], freq[parity][:, CORE:]
        residue = real * real + imag * imag - patterns[:, pl.ds(parity * CORE, CORE)]
        out.append(beside(residue * real, residue * imag))
    real, imag = backward(tables, out)
    up[0] = real
    up[1] = imag

    def gradient(layer):
        f_real, f_imag = field[layer, 0], field[layer, 1]
        u_real, u_imag = up[0], up[1]
        real = f_real * u_real + f_imag * u_imag
        imag = f_real * u_imag - f_imag * u_real
        part[layer, 0] = real[:, :CORE]
        part[layer, 1] = imag[:, :CORE]
        straight, other = real[:, CORE:], turned(imag[:, CORE:])
        send_near[layer] = jnp.where(low, straight, other)
        send_far[layer] = jnp.where(low, other, straight)

    def behind(turn, carry):
        layer = SLICES - 1 - turn
        gradient(layer)
        t_real, t_imag = tile[layer, 0], tile[layer, 1]
        u_real, u_imag = up[0], up[1]
        real, imag = propagate(
            tables, t_real * u_real + t_imag * u_imag, t_real * u_imag - t_imag * u_real, wave, -1
        )
        up[0] = real
        up[1] = imag
        return carry

    lax.fori_loop(0, SLICES - 1, behind, 0)
    gradient(0)


def call(body, outs, scratch=(), smem=1, count=0, limit=8):
    return pl.pallas_call(
        body,
        out_shape=[jax.ShapeDtypeStruct(shape, jnp.float32) for shape in outs],
        in_specs=[pl.BlockSpec(memory_space=pltpu.SMEM)] * smem
        + [pl.BlockSpec(memory_space=pltpu.VMEM)] * count,
        out_specs=[pl.BlockSpec(memory_space=pltpu.VMEM)] * len(outs),
        scratch_shapes=list(scratch),
        compiler_params=pltpu.CompilerParams(vmem_limit_bytes=limit << 20),
        name=body.__name__,
    )


PART = (SLICES, 2, TILE, CORE)
PACK = (SLICES, TILE, CORE)


def step(*args):
    return call(
        step_kernel,
        (PART, PACK, PACK),
        (
            pltpu.VMEM((SLICES, 2, TILE, TILE), jnp.float32),
            pltpu.VMEM((SLICES, 2, TILE, TILE), jnp.float32),
            pltpu.VMEM((2, TILE, TILE), jnp.float32),
        ),
        count=7,
        limit=24,
    )(*args)


def three(value):
    high = value.astype(jnp.bfloat16)
    rest = value - high.astype(jnp.float32)
    middle = rest.astype(jnp.bfloat16)
    low = (rest - middle.astype(jnp.float32)).astype(jnp.bfloat16)
    return high, middle, low


def reorder(order, value):
    high, middle, low = three(value)
    rows = (dot(order[0], high) + dot(order[0], middle)) + dot(order[0], low)
    high, middle, low = three(rows)
    return (dot(high, order[1]) + dot(middle, order[1])) + dot(low, order[1])


def setup_kernel(positions, probe, phase, patterns, order, lit, ordered_phase, ordered_patterns):
    rows = lax.rem(positions[0] + (TILE - MARGIN), TILE)
    cols = lax.rem(positions[1] + (TILE - MARGIN), TILE)
    for part in range(2):
        lit[part] = pltpu.roll(pltpu.roll(probe[part], rows, 0), cols, 1)
    ordered_phase[...] = reorder(order, phase[...])
    ordered_patterns[...] = reorder(order, patterns[...])


def setup(positions, probe, phase, patterns, order):
    shapes = ((2, TILE, TILE), (TILE, TILE), (TILE, TILE))
    return call(setup_kernel, shapes, count=4)(positions, probe, phase, patterns, order)


def pack_columns(even, mid, send_near, send_far):
    low = low_lanes((TILE, CORE)) == even
    for layer in range(SLICES):
        straight, other = mid[layer, 0], turned(mid[layer, 1])
        send_near[layer] = jnp.where(low, other, straight)
        send_far[layer] = jnp.where(low, straight, other)


def assemble_kernel(par, core, near, far, mid, send_near, send_far):
    even = par[0] == 0
    for layer in range(SLICES):
        for part in range(2):
            e, o = near[layer, part], far[layer, part]
            mid[layer, part, :CORE] = core[layer, part]
            mid[layer, part, CORE : CORE + MARGIN] = jnp.where(even, e, o)
            mid[layer, part, CORE + MARGIN :] = jnp.where(even, o, e)
    pack_columns(par[1] == 0, mid, send_near, send_far)


def assemble(*args):
    return call(assemble_kernel, (PART, PACK, PACK), count=3)(*args)


def add_columns(even, part, near, far):
    low = low_lanes((TILE, CORE)) == even
    out = []
    for layer in range(SLICES):
        e, o = near[layer], far[layer]
        out.append(
            (
                part[layer, 0] + jnp.where(low, o, e),
                part[layer, 1] + turned(jnp.where(low, e, o)),
            )
        )
    return out


def share_kernel(par, part, near, far, total, send_near, send_far):
    even = par[0] == 0
    sums = add_columns(par[1] == 0, part, near, far)
    for layer in range(SLICES):
        for c in range(2):
            value = sums[layer][c]
            total[layer, c] = value
            a, b, d, e = (value[k * MARGIN : (k + 1) * MARGIN] for k in range(4))
            send_near[layer, c, :MARGIN] = jnp.where(even, b, e)
            send_near[layer, c, MARGIN:] = jnp.where(even, d, a)
            send_far[layer, c, :MARGIN] = jnp.where(even, e, b)
            send_far[layer, c, MARGIN:] = jnp.where(even, a, d)


def share(*args):
    half = (SLICES, 2, CORE, CORE)
    return call(share_kernel, (PART, half, half), count=3)(*args)


def update_kernel(par, mid, total, near, far, new, send_near, send_far):
    even = par[0] == 0
    above = jnp.where(par[2] == 0, 0.0, STEP_SIZE)
    below = jnp.where(par[3] == 0, 0.0, STEP_SIZE)
    for layer in range(SLICES):
        for c in range(2):
            e, o = near[layer, c], far[layer, c]
            down = jnp.where(even, e, o)
            up = jnp.where(even, o, e)
            for k, (added, scale) in enumerate(
                (
                    (up[MARGIN:], STEP_SIZE),
                    (down[:MARGIN], STEP_SIZE),
                    (down[MARGIN:], below),
                    (up[:MARGIN], above),
                )
            ):
                rows = pl.ds(k * MARGIN, MARGIN)
                new[layer, c, rows] = mid[layer, c, rows] - scale * (total[layer, c, rows] + added)
    pack_columns(par[1] == 0, new, send_near, send_far)


def update(*args):
    return call(update_kernel, (PART, PACK, PACK), count=4)(*args)


def close_kernel(par, part, near, far, total, send_near, send_far):
    even = par[0] == 0
    sums = add_columns(par[1] == 0, part, near, far)
    for layer in range(SLICES):
        for c in range(2):
            value = sums[layer][c]
            total[layer, c] = value[:CORE]
            below, above = value[CORE : CORE + MARGIN], value[CORE + MARGIN :]
            send_near[layer, c] = jnp.where(even, below, above)
            send_far[layer, c] = jnp.where(even, above, below)


def close(*args):
    rim = (SLICES, 2, MARGIN, CORE)
    return call(close_kernel, ((SLICES, 2, CORE, CORE), rim, rim), count=3)(*args)


def finish_kernel(par, mid, total, near, far, out):
    even = par[0] == 0
    for layer in range(SLICES):
        for c in range(2):
            e, o = near[layer, c], far[layer, c]
            for k, added in enumerate((jnp.where(even, o, e), jnp.where(even, e, o))):
                rows = pl.ds(k * MARGIN, MARGIN)
                out[layer, c, rows] = mid[layer, c, rows] - STEP_SIZE * (
                    total[layer, c, rows] + added
                )


def finish(*args):
    return call(finish_kernel, ((SLICES, 2, CORE, CORE),), count=4)(*args)[0]


def swap(axis, near, far):
    count = lax.axis_size(axis)

    def route(first):
        pairs = [(i, i + 1) for i in range(first, count - 1, 2)]
        return pairs + [(j, i) for i, j in pairs]

    far = lax.ppermute(far, axis, route(1))
    near = lax.ppermute(near, axis, route(0))
    return near, far


def shards(object_field, probe, propagator_phase, patterns, scan_positions):
    row, col = lax.axis_index("ty"), lax.axis_index("tx")
    par = jnp.stack([row % 2, col % 2, row, lax.axis_size("ty") - 1 - row]).astype(jnp.int32)
    even = row % 2 == 0
    top, bottom = object_field[:, :, :MARGIN], object_field[:, :, MARGIN:]
    near, far = swap("ty", jnp.where(even, bottom, top), jnp.where(even, top, bottom))
    lit, phase, ordered = setup(
        scan_positions[0, 0, 0], probe, propagator_phase, patterns[0, 0, 0], order_table()
    )
    wave = jnp.stack([jnp.cos(phase), jnp.sin(phase)])
    tables = jnp.asarray(half_tables())
    mid, near, far = assemble(par, object_field, near, far)
    for turn in range(STEPS):
        near, far = swap("tx", near, far)
        part, near, far = step(par, mid, near, far, lit, wave, ordered, tables)
        near, far = swap("tx", near, far)
        if turn < STEPS - 1:
            total, near, far = share(par, part, near, far)
            near, far = swap("ty", near, far)
            mid, near, far = update(par, mid, total, near, far)
    total, near, far = close(par, part, near, far)
    near, far = swap("ty", near, far)
    return finish(par, mid, total, near, far)


def solution(mesh):
    placed = (
        P(None, None, "ty", "tx"),
        P(),
        P(),
        P("ty", "tx", None, None, None),
        P("ty", "tx", None, None),
    )
    return jax.shard_map(
        shards, mesh=mesh, in_specs=placed, out_specs=P(None, None, "ty", "tx"), check_vma=False
    )
```

```python
import functools
import math

import jax
import jax.numpy as jnp
import numpy as np
from jax import lax
from jax.experimental import pallas as pl
from jax.experimental.pallas import tpu as pltpu
from jax.sharding import PartitionSpec as P

MARGIN = 64
CORE = 128
TILE = 256
SLICES = 3
STEPS = 2
STEP_SIZE = 0.05


def half_tables():
    index = np.arange(CORE)
    tables = []
    for parity in range(2):
        freq = 2 * index + parity
        angle = 2.0 * math.pi * ((freq[:, None] * index[None, :]) % TILE) / TILE
        real, imag = np.cos(angle) / 16.0, -np.sin(angle) / 16.0
        block = np.block([[real, -imag], [imag, real]]).astype(np.float32)
        for table in (block, block.T):
            high = table.astype(jnp.bfloat16)
            low = (table - high.astype(np.float32)).astype(jnp.bfloat16)
            tables.append(np.stack([high, low]))
    return np.stack(tables)


def order_table():
    table = np.zeros((TILE, TILE), np.float32)
    index = np.arange(CORE)
    table[index, 2 * index] = 1.0
    table[CORE + index, 2 * index + 1] = 1.0
    return np.stack([table, table.T]).astype(jnp.bfloat16)


def dot(left, right):
    return jnp.dot(left, right, preferred_element_type=jnp.float32)


def split(value):
    high = value.astype(jnp.bfloat16)
    low = (value - high.astype(jnp.float32)).astype(jnp.bfloat16)
    return high, low


def from_left(tables, which, value):
    high, low = split(value)
    t_high, t_low = tables[which, 0], tables[which, 1]
    return dot(t_high, high) + (dot(t_high, low) + dot(t_low, high))


def from_right(tables, which, value):
    high, low = split(value)
    t_high, t_low = tables[which, 0], tables[which, 1]
    return dot(high, t_high) + (dot(high, t_low) + dot(low, t_high))


def stack(*rows):
    return jnp.concatenate(rows, axis=0)


def beside(*cols):
    return jnp.concatenate(cols, axis=1)


def forward(tables, real, imag):
    half = []
    for parity in range(2):
        if parity == 0:
            mixed = stack(real[:CORE] + real[CORE:], imag[:CORE] + imag[CORE:])
        else:
            mixed = stack(real[:CORE] - real[CORE:], imag[:CORE] - imag[CORE:])
        half.append(from_left(tables, 2 * parity, mixed))
    out = []
    for parity in range(2):
        rows = []
        for value in half:
            parts = []
            for part in (value[:CORE], value[CORE:]):
                first, second = part[:, :CORE], part[:, CORE:]
                parts.append(first + second if parity == 0 else first - second)
            rows.append(beside(*parts))
        out.append(from_right(tables, 2 * parity + 1, stack(*rows)))
    return out


def backward(tables, freq):
    even = from_right(tables, 0, freq[0])
    odd = from_right(tables, 2, freq[1])
    first, second = even + odd, even - odd
    half = []
    for parity in range(2):
        rows = slice(parity * CORE, (parity + 1) * CORE)
        mixed = stack(
            beside(first[rows, :CORE], second[rows, :CORE]),
            beside(first[rows, CORE:], second[rows, CORE:]),
        )
        half.append(from_left(tables, 2 * parity + 1, mixed))
    even, odd = half
    real = stack(even[:CORE] + odd[:CORE], even[:CORE] - odd[:CORE])
    imag = stack(even[CORE:] + odd[CORE:], even[CORE:] - odd[CORE:])
    return real, imag


def propagate(tables, real, imag, wave, sign):
    freq = forward(tables, real, imag)
    out = []
    for parity in range(2):
        real, imag = freq[parity][:, :CORE], freq[parity][:, CORE:]
        cols = pl.ds(parity * CORE, CORE)
        h_real, h_imag = wave[0, :, cols], wave[1, :, cols]
        if sign < 0:
            out.append(beside(real * h_real + imag * h_imag, imag * h_real - real * h_imag))
        else:
            out.append(beside(real * h_real - imag * h_imag, imag * h_real + real * h_imag))
    return backward(tables, out)


def low_lanes(shape):
    return lax.broadcasted_iota(jnp.int32, shape, len(shape) - 1) < MARGIN


def turned(value):
    return pltpu.roll(value, MARGIN, 1)


def near_lanes(par, rows):
    return low_lanes((rows, CORE)) != (par[1] == 0)


def pack(nearby, real, imag):
    other = turned(imag)
    return jnp.where(nearby, real, other), jnp.where(nearby, other, real)


def unpack(nearby, first, second):
    return jnp.where(nearby, first, second), turned(jnp.where(nearby, second, first))


def step_kernel(
    par,
    first,
    second,
    near,
    far,
    lit,
    wave,
    patterns,
    tables,
    part_first,
    part_second,
    send_near,
    send_far,
    tile,
    field,
    up,
):
    nearby = near_lanes(par, TILE)
    for layer in range(SLICES):
        real, imag = unpack(nearby, first[layer], second[layer])
        tile[layer, 0, :, :CORE] = real
        tile[layer, 1, :, :CORE] = imag
        real, imag = unpack(nearby, far[layer], near[layer])
        tile[layer, 0, :, CORE:] = real
        tile[layer, 1, :, CORE:] = imag
    field[0, 0] = lit[0]
    field[0, 1] = lit[1]

    def ahead(layer, carry):
        f_real, f_imag = field[layer, 0], field[layer, 1]
        t_real, t_imag = tile[layer, 0], tile[layer, 1]
        real, imag = propagate(
            tables, f_real * t_real - f_imag * t_imag, f_real * t_imag + f_imag * t_real, wave, 1
        )
        field[layer + 1, 0] = real
        field[layer + 1, 1] = imag
        return carry

    lax.fori_loop(0, SLICES - 1, ahead, 0)
    f_real, f_imag = field[SLICES - 1, 0], field[SLICES - 1, 1]
    t_real, t_imag = tile[SLICES - 1, 0], tile[SLICES - 1, 1]
    freq = forward(tables, f_real * t_real - f_imag * t_imag, f_real * t_imag + f_imag * t_real)
    out = []
    for parity in range(2):
        real, imag = freq[parity][:, :CORE], freq[parity][:, CORE:]
        residue = real * real + imag * imag - patterns[:, pl.ds(parity * CORE, CORE)]
        out.append(beside(residue * real, residue * imag))
    real, imag = backward(tables, out)
    up[0] = real
    up[1] = imag

    def gradient(layer):
        f_real, f_imag = field[layer, 0], field[layer, 1]
        u_real, u_imag = up[0], up[1]
        real = f_real * u_real + f_imag * u_imag
        imag = f_real * u_imag - f_imag * u_real
        part_first[layer], part_second[layer] = pack(nearby, real[:, :CORE], imag[:, :CORE])
        send_far[layer], send_near[layer] = pack(nearby, real[:, CORE:], imag[:, CORE:])

    def behind(turn, carry):
        layer = SLICES - 1 - turn
        gradient(layer)
        t_real, t_imag = tile[layer, 0], tile[layer, 1]
        u_real, u_imag = up[0], up[1]
        real, imag = propagate(
            tables, t_real * u_real + t_imag * u_imag, t_real * u_imag - t_imag * u_real, wave, -1
        )
        up[0] = real
        up[1] = imag
        return carry

    lax.fori_loop(0, SLICES - 1, behind, 0)
    gradient(0)


def call(body, outs, scratch=(), smem=1, count=0, limit=8):
    return pl.pallas_call(
        body,
        out_shape=[jax.ShapeDtypeStruct(shape, jnp.float32) for shape in outs],
        in_specs=[pl.BlockSpec(memory_space=pltpu.SMEM)] * smem
        + [pl.BlockSpec(memory_space=pltpu.VMEM)] * count,
        out_specs=[pl.BlockSpec(memory_space=pltpu.VMEM)] * len(outs),
        scratch_shapes=list(scratch),
        compiler_params=pltpu.CompilerParams(vmem_limit_bytes=limit << 20),
        name=body.__name__,
    )


PACK = (SLICES, TILE, CORE)
HALF = (SLICES, CORE, CORE)
RIMS = (2, SLICES, MARGIN, CORE)


def step(*args):
    return call(
        step_kernel,
        (PACK, PACK, PACK, PACK),
        (
            pltpu.VMEM((SLICES, 2, TILE, TILE), jnp.float32),
            pltpu.VMEM((SLICES, 2, TILE, TILE), jnp.float32),
            pltpu.VMEM((2, TILE, TILE), jnp.float32),
        ),
        count=8,
        limit=24,
    )(*args)


def three(value):
    high = value.astype(jnp.bfloat16)
    rest = value - high.astype(jnp.float32)
    middle = rest.astype(jnp.bfloat16)
    low = (rest - middle.astype(jnp.float32)).astype(jnp.bfloat16)
    return high, middle, low


def reorder(order, value):
    high, middle, low = three(value)
    rows = (dot(order[0], high) + dot(order[0], middle)) + dot(order[0], low)
    high, middle, low = three(rows)
    return (dot(high, order[1]) + dot(middle, order[1])) + dot(low, order[1])


def setup_kernel(positions, probe, phase, patterns, order, lit, ordered_phase, ordered_patterns):
    rows = lax.rem(positions[0] + (TILE - MARGIN), TILE)
    cols = lax.rem(positions[1] + (TILE - MARGIN), TILE)
    for part in range(2):
        lit[part] = pltpu.roll(pltpu.roll(probe[part], rows, 0), cols, 1)
    ordered_phase[...] = reorder(order, phase[...])
    ordered_patterns[...] = reorder(order, patterns[...])


def setup(positions, probe, phase, patterns, order):
    shapes = ((2, TILE, TILE), (TILE, TILE), (TILE, TILE))
    return call(setup_kernel, shapes, count=4)(positions, probe, phase, patterns, order)


def open_kernel(par, core, first, second, near, far):
    even = par[0] == 0
    nearby = near_lanes(par, CORE)
    for layer in range(SLICES):
        packs = pack(nearby, core[layer, 0], core[layer, 1])
        for k, (value, whole) in enumerate(zip(packs, (first, second))):
            whole[layer] = value
            near[k, layer] = jnp.where(even, value[MARGIN:], value[:MARGIN])
            far[k, layer] = jnp.where(even, value[:MARGIN], value[MARGIN:])


def begin(par, core):
    return call(open_kernel, (HALF, HALF, RIMS, RIMS), count=1)(par, core)


def assemble_kernel(par, core_1, core_2, near, far, first, second):
    even = par[0] == 0
    for k, (core, mid) in enumerate(((core_1, first), (core_2, second))):
        for layer in range(SLICES):
            mid[layer, :CORE] = core[layer]
            mid[layer, CORE : CORE + MARGIN] = jnp.where(even, near[k, layer], far[k, layer])
            mid[layer, CORE + MARGIN :] = jnp.where(even, far[k, layer], near[k, layer])


def assemble(*args):
    return call(assemble_kernel, (PACK, PACK), count=4)(*args)


def share_kernel(par, part, came, total, send_near, send_far):
    even = par[0] == 0
    for layer in range(SLICES):
        value = part[layer] + came[layer]
        total[layer] = value
        a, b, d, e = (value[k * MARGIN : (k + 1) * MARGIN] for k in range(4))
        send_near[layer, :MARGIN] = jnp.where(even, b, e)
        send_near[layer, MARGIN:] = jnp.where(even, d, a)
        send_far[layer, :MARGIN] = jnp.where(even, e, b)
        send_far[layer, MARGIN:] = jnp.where(even, a, d)


def share(*args):
    return call(share_kernel, (PACK, HALF, HALF), count=2)(*args)


def update_kernel(par, mid, total, near, far, new):
    even = par[0] == 0
    above = jnp.where(par[2] == 0, 0.0, STEP_SIZE)
    below = jnp.where(par[3] == 0, 0.0, STEP_SIZE)
    for layer in range(SLICES):
        e, o = near[layer], far[layer]
        down = jnp.where(even, e, o)
        up = jnp.where(even, o, e)
        for k, (added, scale) in enumerate(
            (
                (up[MARGIN:], STEP_SIZE),
                (down[:MARGIN], STEP_SIZE),
                (down[MARGIN:], below),
                (up[:MARGIN], above),
            )
        ):
            rows = pl.ds(k * MARGIN, MARGIN)
            new[layer, rows] = mid[layer, rows] - scale * (total[layer, rows] + added)


def update(*args):
    return call(update_kernel, (PACK,), count=4)(*args)[0]


def close_kernel(par, part_1, part_2, came_1, came_2, total, send_near, send_far):
    even = par[0] == 0
    for k, (part, came) in enumerate(((part_1, came_1), (part_2, came_2))):
        for layer in range(SLICES):
            value = part[layer] + came[layer]
            total[k, layer] = value[:CORE]
            below, above = value[CORE : CORE + MARGIN], value[CORE + MARGIN :]
            send_near[k, layer] = jnp.where(even, below, above)
            send_far[k, layer] = jnp.where(even, above, below)


def close(*args):
    return call(close_kernel, ((2, *HALF), RIMS, RIMS), count=4)(*args)


def finish_kernel(par, mid_1, mid_2, total, near, far, out):
    even = par[0] == 0
    nearby = near_lanes(par, MARGIN)
    for layer in range(SLICES):
        for half in range(2):
            rows = pl.ds(half * MARGIN, MARGIN)
            packs = []
            for k, mid in enumerate((mid_1, mid_2)):
                e, o = near[k, layer], far[k, layer]
                added = jnp.where(even, o, e) if half == 0 else jnp.where(even, e, o)
                packs.append(mid[layer, rows] - STEP_SIZE * (total[k, layer, rows] + added))
            out[layer, 0, rows], out[layer, 1, rows] = unpack(nearby, *packs)


def finish(*args):
    return call(finish_kernel, ((SLICES, 2, CORE, CORE),), count=5)(*args)[0]


def swap(axis, first, block):
    count = lax.axis_size(axis)
    pairs = [(i, i + 1) for i in range(first, count - 1, 2)]
    return lax.ppermute(block, axis, pairs + [(j, i) for i, j in pairs])


def swap_rows(near, far):
    far = swap("ty", 1, far)
    return swap("ty", 0, near), far


def shards(object_field, probe, propagator_phase, patterns, scan_positions):
    row, col = lax.axis_index("ty"), lax.axis_index("tx")
    par = jnp.stack([row % 2, col % 2, row, lax.axis_size("ty") - 1 - row]).astype(jnp.int32)
    first, second, near, far = begin(par, object_field)
    near, far = swap_rows(near, far)
    lit, phase, ordered = setup(
        scan_positions[0, 0, 0], probe, propagator_phase, patterns[0, 0, 0], order_table()
    )
    wave = jnp.stack([jnp.cos(phase), jnp.sin(phase)])
    tables = jnp.asarray(half_tables())
    first, second = assemble(par, first, second, near, far)
    for turn in range(STEPS):
        far = swap("tx", 1, second)
        near = swap("tx", 0, first)
        part_1, part_2, near, far = step(
            par, first, second, near, far, lit, wave, ordered, tables
        )
        far = swap("tx", 1, far)
        near = swap("tx", 0, near)
        if turn < STEPS - 1:
            total_1, near_1, far_1 = share(par, part_1, near)
            near_1, far_1 = swap_rows(near_1, far_1)
            total_2, near_2, far_2 = share(par, part_2, far)
            near_2, far_2 = swap_rows(near_2, far_2)
            first = update(par, first, total_1, near_1, far_1)
            second = update(par, second, total_2, near_2, far_2)
    total, near, far = close(par, part_1, part_2, near, far)
    near, far = swap_rows(near, far)
    return finish(par, first, second, total, near, far)


def solution(mesh):
    placed = (
        P(None, None, "ty", "tx"),
        P(),
        P(),
        P("ty", "tx", None, None, None),
        P("ty", "tx", None, None),
    )
    return jax.shard_map(
        shards, mesh=mesh, in_specs=placed, out_specs=P(None, None, "ty", "tx"), check_vma=False
    )
```

```python
import math

import jax
import jax.numpy as jnp
import numpy as np
from jax import lax
from jax.experimental import pallas as pl
from jax.experimental.pallas import tpu as pltpu
from jax.sharding import PartitionSpec as P


MARGIN = 64
CORE = 128
TILE = 256
SLICES = 3
STEPS = 2
STEP_SIZE = 0.05


def half_tables():
    index = np.arange(CORE)
    tables = []
    for parity in range(2):
        freq = 2 * index + parity
        angle = 2.0 * math.pi * ((freq[:, None] * index[None, :]) % TILE) / TILE
        real, imag = np.cos(angle) / 16.0, -np.sin(angle) / 16.0
        block = np.block([[real, -imag], [imag, real]]).astype(np.float32)
        for table in (block, block.T):
            high = table.astype(jnp.bfloat16)
            low = (table - high.astype(np.float32)).astype(jnp.bfloat16)
            tables.append(np.stack([high, low]))
    return np.stack(tables)


def order_table():
    table = np.zeros((TILE, TILE), np.float32)
    index = np.arange(CORE)
    table[index, 2 * index] = 1.0
    table[CORE + index, 2 * index + 1] = 1.0
    return np.stack([table, table.T]).astype(jnp.bfloat16)


def dot(left, right):
    return jnp.dot(left, right, preferred_element_type=jnp.float32)


def split(value):
    high = value.astype(jnp.bfloat16)
    low = (value - high.astype(jnp.float32)).astype(jnp.bfloat16)
    return high, low


def from_left(tables, which, value):
    high, low = split(value)
    both = dot(tables[which].reshape(2 * TILE, TILE), high)
    return both[:TILE] + (both[TILE:] + dot(tables[which, 0], low))


def from_right(tables, which, value):
    high, low = split(value)
    both = dot(jnp.concatenate([high, low], axis=0), tables[which, 0])
    return both[:TILE] + (both[TILE:] + dot(high, tables[which, 1]))


def stack(*rows):
    return jnp.concatenate(rows, axis=0)


def beside(*cols):
    return jnp.concatenate(cols, axis=1)


def forward(tables, real, imag):
    half = []
    for parity in range(2):
        if parity == 0:
            mixed = stack(real[:CORE] + real[CORE:], imag[:CORE] + imag[CORE:])
        else:
            mixed = stack(real[:CORE] - real[CORE:], imag[:CORE] - imag[CORE:])
        half.append(from_left(tables, 2 * parity, mixed))
    out = []
    for parity in range(2):
        rows = []
        for value in half:
            parts = []
            for part in (value[:CORE], value[CORE:]):
                first, second = part[:, :CORE], part[:, CORE:]
                parts.append(first + second if parity == 0 else first - second)
            rows.append(beside(*parts))
        out.append(from_right(tables, 2 * parity + 1, stack(*rows)))
    return out


def backward(tables, freq):
    even = from_right(tables, 0, freq[0])
    odd = from_right(tables, 2, freq[1])
    first, second = even + odd, even - odd
    half = []
    for parity in range(2):
        rows = slice(parity * CORE, (parity + 1) * CORE)
        mixed = stack(
            beside(first[rows, :CORE], second[rows, :CORE]),
            beside(first[rows, CORE:], second[rows, CORE:]),
        )
        half.append(from_left(tables, 2 * parity + 1, mixed))
    even, odd = half
    real = stack(even[:CORE] + odd[:CORE], even[:CORE] - odd[:CORE])
    imag = stack(even[CORE:] + odd[CORE:], even[CORE:] - odd[CORE:])
    return real, imag


def propagate(tables, real, imag, wave, sign):
    freq = forward(tables, real, imag)
    out = []
    for parity in range(2):
        real, imag = freq[parity][:, :CORE], freq[parity][:, CORE:]
        cols = pl.ds(parity * CORE, CORE)
        h_real, h_imag = wave[0, :, cols], wave[1, :, cols]
        if sign < 0:
            out.append(beside(real * h_real + imag * h_imag, imag * h_real - real * h_imag))
        else:
            out.append(beside(real * h_real - imag * h_imag, imag * h_real + real * h_imag))
    return backward(tables, out)


def low_lanes(shape):
    return lax.broadcasted_iota(jnp.int32, shape, len(shape) - 1) < MARGIN


def turned(value):
    return pltpu.roll(value, MARGIN, 1)


def near_lanes(par, rows):
    return low_lanes((rows, CORE)) != (par[1] == 0)


def pack(nearby, real, imag):
    other = turned(imag)
    return jnp.where(nearby, real, other), jnp.where(nearby, other, real)


def unpack(nearby, first, second):
    return jnp.where(nearby, first, second), turned(jnp.where(nearby, second, first))


def step_kernel(
    par,
    first,
    second,
    near,
    far,
    lit,
    wave,
    patterns,
    tables,
    part_first,
    part_second,
    send_near,
    send_far,
    tile,
    field,
):
    nearby = near_lanes(par, TILE)
    for layer in range(SLICES):
        real, imag = unpack(nearby, first[layer], second[layer])
        tile[layer, 0, :, :CORE] = real
        tile[layer, 1, :, :CORE] = imag
        real, imag = unpack(nearby, far[layer], near[layer])
        tile[layer, 0, :, CORE:] = real
        tile[layer, 1, :, CORE:] = imag
    f_real, f_imag = lit[0], lit[1]
    for layer in range(SLICES - 1):
        t_real, t_imag = tile[layer, 0], tile[layer, 1]
        f_real, f_imag = propagate(
            tables, f_real * t_real - f_imag * t_imag, f_real * t_imag + f_imag * t_real, wave, 1
        )
        field[layer, 0] = f_real
        field[layer, 1] = f_imag
    t_real, t_imag = tile[SLICES - 1, 0], tile[SLICES - 1, 1]
    freq = forward(tables, f_real * t_real - f_imag * t_imag, f_real * t_imag + f_imag * t_real)
    out = []
    for parity in range(2):
        real, imag = freq[parity][:, :CORE], freq[parity][:, CORE:]
        residue = real * real + imag * imag - patterns[:, pl.ds(parity * CORE, CORE)]
        out.append(beside(residue * real, residue * imag))
    u_real, u_imag = backward(tables, out)
    for layer in reversed(range(SLICES)):
        if layer > 0:
            f_real, f_imag = field[layer - 1, 0], field[layer - 1, 1]
        else:
            f_real, f_imag = lit[0], lit[1]
        real = f_real * u_real + f_imag * u_imag
        imag = f_real * u_imag - f_imag * u_real
        part_first[layer], part_second[layer] = pack(nearby, real[:, :CORE], imag[:, :CORE])
        send_far[layer], send_near[layer] = pack(nearby, real[:, CORE:], imag[:, CORE:])
        if layer > 0:
            t_real, t_imag = tile[layer, 0], tile[layer, 1]
            u_real, u_imag = propagate(
                tables,
                t_real * u_real + t_imag * u_imag,
                t_real * u_imag - t_imag * u_real,
                wave,
                -1,
            )


def call(body, outs, scratch=(), smem=1, count=0, limit=8):
    return pl.pallas_call(
        body,
        out_shape=[jax.ShapeDtypeStruct(shape, jnp.float32) for shape in outs],
        in_specs=[pl.BlockSpec(memory_space=pltpu.SMEM)] * smem
        + [pl.BlockSpec(memory_space=pltpu.VMEM)] * count,
        out_specs=[pl.BlockSpec(memory_space=pltpu.VMEM)] * len(outs),
        scratch_shapes=list(scratch),
        compiler_params=pltpu.CompilerParams(vmem_limit_bytes=limit << 20),
    )


PACK = (SLICES, TILE, CORE)
HALF = (SLICES, CORE, CORE)
RIMS = (2, SLICES, MARGIN, CORE)


def step(*args):
    return call(
        step_kernel,
        (PACK, PACK, PACK, PACK),
        (
            pltpu.VMEM((SLICES, 2, TILE, TILE), jnp.float32),
            pltpu.VMEM((SLICES - 1, 2, TILE, TILE), jnp.float32),
        ),
        count=8,
        limit=24,
    )(*args)


def three(value):
    high = value.astype(jnp.bfloat16)
    rest = value - high.astype(jnp.float32)
    middle = rest.astype(jnp.bfloat16)
    low = (rest - middle.astype(jnp.float32)).astype(jnp.bfloat16)
    return high, middle, low


def reorder(order, value):
    high, middle, low = three(value)
    rows = (dot(order[0], high) + dot(order[0], middle)) + dot(order[0], low)
    high, middle, low = three(rows)
    return (dot(high, order[1]) + dot(middle, order[1])) + dot(low, order[1])


def setup_kernel(positions, probe, phase, patterns, order, lit, ordered_phase, ordered_patterns):
    rows = lax.rem(positions[0] + (TILE - MARGIN), TILE)
    cols = lax.rem(positions[1] + (TILE - MARGIN), TILE)
    for part in range(2):
        lit[part] = pltpu.roll(pltpu.roll(probe[part], rows, 0), cols, 1)
    ordered_phase[...] = reorder(order, phase[...])
    ordered_patterns[...] = reorder(order, patterns[...])


def setup(positions, probe, phase, patterns, order):
    shapes = ((2, TILE, TILE), (TILE, TILE), (TILE, TILE))
    return call(setup_kernel, shapes, count=4)(positions, probe, phase, patterns, order)


def open_kernel(par, core, first, second, near, far):
    even = par[0] == 0
    nearby = near_lanes(par, CORE)
    for layer in range(SLICES):
        packs = pack(nearby, core[layer, 0], core[layer, 1])
        for k, (value, whole) in enumerate(zip(packs, (first, second))):
            whole[layer] = value
            near[k, layer] = jnp.where(even, value[MARGIN:], value[:MARGIN])
            far[k, layer] = jnp.where(even, value[:MARGIN], value[MARGIN:])


def begin(par, core):
    return call(open_kernel, (HALF, HALF, RIMS, RIMS), count=1)(par, core)


def assemble_kernel(par, core_1, core_2, near, far, first, second):
    even = par[0] == 0
    for k, (core, mid) in enumerate(((core_1, first), (core_2, second))):
        for layer in range(SLICES):
            mid[layer, :CORE] = core[layer]
            mid[layer, CORE : CORE + MARGIN] = jnp.where(even, near[k, layer], far[k, layer])
            mid[layer, CORE + MARGIN :] = jnp.where(even, far[k, layer], near[k, layer])


def assemble(*args):
    return call(assemble_kernel, (PACK, PACK), count=4)(*args)


def share_kernel(par, part_1, part_2, came_1, came_2, total, send_near, send_far):
    even = par[0] == 0
    for k, (part, came) in enumerate(((part_1, came_1), (part_2, came_2))):
        for layer in range(SLICES):
            value = part[layer] + came[layer]
            total[k, layer] = value
            a, b, d, e = (value[n * MARGIN : (n + 1) * MARGIN] for n in range(4))
            send_near[k, layer, :MARGIN] = jnp.where(even, b, e)
            send_near[k, layer, MARGIN:] = jnp.where(even, d, a)
            send_far[k, layer, :MARGIN] = jnp.where(even, e, b)
            send_far[k, layer, MARGIN:] = jnp.where(even, a, d)


def share(*args):
    return call(share_kernel, ((2, *PACK), (2, *HALF), (2, *HALF)), count=4)(*args)


def update_kernel(par, mid_1, mid_2, total, near, far, new_1, new_2):
    even = par[0] == 0
    above = jnp.where(par[2] == 0, 0.0, STEP_SIZE)
    below = jnp.where(par[3] == 0, 0.0, STEP_SIZE)
    for k, (mid, new) in enumerate(((mid_1, new_1), (mid_2, new_2))):
        for layer in range(SLICES):
            e, o = near[k, layer], far[k, layer]
            down = jnp.where(even, e, o)
            up = jnp.where(even, o, e)
            for n, (added, scale) in enumerate(
                (
                    (up[MARGIN:], STEP_SIZE),
                    (down[:MARGIN], STEP_SIZE),
                    (down[MARGIN:], below),
                    (up[:MARGIN], above),
                )
            ):
                rows = pl.ds(n * MARGIN, MARGIN)
                new[layer, rows] = mid[layer, rows] - scale * (total[k, layer, rows] + added)


def update(*args):
    return call(update_kernel, (PACK, PACK), count=5)(*args)


def close_kernel(par, part_1, part_2, came_1, came_2, total, send_near, send_far):
    even = par[0] == 0
    for k, (part, came) in enumerate(((part_1, came_1), (part_2, came_2))):
        for layer in range(SLICES):
            value = part[layer] + came[layer]
            total[k, layer] = value[:CORE]
            below, above = value[CORE : CORE + MARGIN], value[CORE + MARGIN :]
            send_near[k, layer] = jnp.where(even, below, above)
            send_far[k, layer] = jnp.where(even, above, below)


def close(*args):
    return call(close_kernel, ((2, *HALF), RIMS, RIMS), count=4)(*args)


def finish_kernel(par, mid_1, mid_2, total, near, far, out):
    even = par[0] == 0
    nearby = near_lanes(par, MARGIN)
    for layer in range(SLICES):
        for half in range(2):
            rows = pl.ds(half * MARGIN, MARGIN)
            packs = []
            for k, mid in enumerate((mid_1, mid_2)):
                e, o = near[k, layer], far[k, layer]
                added = jnp.where(even, o, e) if half == 0 else jnp.where(even, e, o)
                packs.append(mid[layer, rows] - STEP_SIZE * (total[k, layer, rows] + added))
            out[layer, 0, rows], out[layer, 1, rows] = unpack(nearby, *packs)


def finish(*args):
    return call(finish_kernel, ((SLICES, 2, CORE, CORE),), count=5)(*args)[0]


def swap(axis, first, block):
    count = lax.axis_size(axis)
    pairs = [(i, i + 1) for i in range(first, count - 1, 2)]
    return lax.ppermute(block, axis, pairs + [(j, i) for i, j in pairs])


def swap_rows(near, far):
    far = swap("ty", 1, far)
    near = swap("ty", 0, near)
    return near, far


def exchange_and_step(object_field, probe, propagator_phase, patterns, scan_positions):
    row, col = lax.axis_index("ty"), lax.axis_index("tx")
    par = jnp.stack([row % 2, col % 2, row, lax.axis_size("ty") - 1 - row]).astype(jnp.int32)
    first, second, near, far = begin(par, object_field)
    near, far = swap_rows(near, far)
    lit, phase, ordered = setup(
        scan_positions[0, 0, 0], probe, propagator_phase, patterns[0, 0, 0], order_table()
    )
    wave = jnp.stack([jnp.cos(phase), jnp.sin(phase)])
    tables = jnp.asarray(half_tables())
    first, second = assemble(par, first, second, near, far)
    for turn in range(STEPS):
        far = swap("tx", 1, second)
        near = swap("tx", 0, first)
        part_1, part_2, near, far = step(
            par, first, second, near, far, lit, wave, ordered, tables
        )
        far = swap("tx", 1, far)
        near = swap("tx", 0, near)
        if turn < STEPS - 1:
            total, near, far = share(par, part_1, part_2, near, far)
            near, far = swap_rows(near, far)
            first, second = update(par, first, second, total, near, far)
    total, near, far = close(par, part_1, part_2, near, far)
    near, far = swap_rows(near, far)
    return finish(par, first, second, total, near, far)


def solution(mesh):
    placed = (
        P(None, None, "ty", "tx"),
        P(),
        P(),
        P("ty", "tx", None, None, None),
        P("ty", "tx", None, None),
    )
    return jax.shard_map(
        exchange_and_step, mesh=mesh, in_specs=placed, out_specs=P(None, None, "ty", "tx"), check_vma=False
    )
```

```python
import functools
import math

import jax
import jax.numpy as jnp
import numpy as np
from jax import lax
from jax.experimental import pallas as pl
from jax.experimental.pallas import tpu as pltpu
from jax.sharding import PartitionSpec as P

MARGIN = 64
CORE = 128
TILE = 256
SLICES = 3
STEPS = 2
STEP_SIZE = 0.05


def half_tables():
    index = np.arange(CORE)
    tables = []
    for parity in range(2):
        freq = 2 * index + parity
        angle = 2.0 * math.pi * ((freq[:, None] * index[None, :]) % TILE) / TILE
        real, imag = np.cos(angle) / 16.0, -np.sin(angle) / 16.0
        block = np.block([[real, -imag], [imag, real]]).astype(np.float32)
        for table in (block, block.T):
            high = table.astype(jnp.bfloat16)
            low = (table - high.astype(np.float32)).astype(jnp.bfloat16)
            tables.append(np.stack([high, low]))
    return np.stack(tables)


def order_table():
    table = np.zeros((TILE, TILE), np.float32)
    index = np.arange(CORE)
    table[index, 2 * index] = 1.0
    table[CORE + index, 2 * index + 1] = 1.0
    return np.stack([table, table.T]).astype(jnp.bfloat16)


def dot(left, right):
    return jnp.dot(left, right, preferred_element_type=jnp.float32)


def split(value):
    high = value.astype(jnp.bfloat16)
    low = (value - high.astype(jnp.float32)).astype(jnp.bfloat16)
    return high, low


def from_left(tables, which, value):
    high, low = split(value)
    both = dot(tables[which].reshape(2 * TILE, TILE), high)
    return both[:TILE] + (both[TILE:] + dot(tables[which, 0], low))


def from_right(tables, which, value):
    high, low = split(value)
    both = dot(jnp.concatenate([high, low], axis=0), tables[which, 0])
    return both[:TILE] + (both[TILE:] + dot(high, tables[which, 1]))


def stack(*rows):
    return jnp.concatenate(rows, axis=0)


def beside(*cols):
    return jnp.concatenate(cols, axis=1)


def forward(tables, real, imag):
    half = []
    for parity in range(2):
        if parity == 0:
            mixed = stack(real[:CORE] + real[CORE:], imag[:CORE] + imag[CORE:])
        else:
            mixed = stack(real[:CORE] - real[CORE:], imag[:CORE] - imag[CORE:])
        half.append(from_left(tables, 2 * parity, mixed))
    out = []
    for parity in range(2):
        rows = []
        for value in half:
            parts = []
            for part in (value[:CORE], value[CORE:]):
                first, second = part[:, :CORE], part[:, CORE:]
                parts.append(first + second if parity == 0 else first - second)
            rows.append(beside(*parts))
        out.append(from_right(tables, 2 * parity + 1, stack(*rows)))
    return out


def backward(tables, freq):
    even = from_right(tables, 0, freq[0])
    odd = from_right(tables, 2, freq[1])
    first, second = even + odd, even - odd
    half = []
    for parity in range(2):
        rows = slice(parity * CORE, (parity + 1) * CORE)
        mixed = stack(
            beside(first[rows, :CORE], second[rows, :CORE]),
            beside(first[rows, CORE:], second[rows, CORE:]),
        )
        half.append(from_left(tables, 2 * parity + 1, mixed))
    even, odd = half
    real = stack(even[:CORE] + odd[:CORE], even[:CORE] - odd[:CORE])
    imag = stack(even[CORE:] + odd[CORE:], even[CORE:] - odd[CORE:])
    return real, imag


def propagate(tables, real, imag, wave, sign):
    freq = forward(tables, real, imag)
    out = []
    for parity in range(2):
        real, imag = freq[parity][:, :CORE], freq[parity][:, CORE:]
        cols = pl.ds(parity * CORE, CORE)
        h_real, h_imag = wave[0, :, cols], wave[1, :, cols]
        if sign < 0:
            out.append(beside(real * h_real + imag * h_imag, imag * h_real - real * h_imag))
        else:
            out.append(beside(real * h_real - imag * h_imag, imag * h_real + real * h_imag))
    return backward(tables, out)


def even_row():
    return lax.rem(lax.axis_index("ty"), 2) == 0


def low_lanes(shape):
    return lax.broadcasted_iota(jnp.int32, shape, len(shape) - 1) < MARGIN


def turned(value):
    return pltpu.roll(value, MARGIN, 1)


def near_lanes(rows):
    return low_lanes((rows, CORE)) != (lax.rem(lax.axis_index("tx"), 2) == 0)


def pack(nearby, real, imag):
    other = turned(imag)
    return jnp.where(nearby, real, other), jnp.where(nearby, other, real)


def unpack(nearby, first, second):
    return jnp.where(nearby, first, second), turned(jnp.where(nearby, second, first))


def step_kernel(
    first,
    second,
    near,
    far,
    lit,
    wave,
    patterns,
    tables,
    part_first,
    part_second,
    send_near,
    send_far,
    tile,
    field,
):
    nearby = near_lanes(TILE)

    for layer in range(SLICES):
        core = unpack(nearby, first[layer], second[layer])
        margin = unpack(nearby, far[layer], near[layer])
        for c in range(2):
            tile[layer, c] = beside(core[c], margin[c])
    f_real, f_imag = lit[0], lit[1]
    for layer in range(SLICES - 1):
        t_real, t_imag = tile[layer, 0], tile[layer, 1]
        f_real, f_imag = propagate(
            tables, f_real * t_real - f_imag * t_imag, f_real * t_imag + f_imag * t_real, wave, 1
        )
        field[layer, 0] = f_real
        field[layer, 1] = f_imag
    t_real, t_imag = tile[SLICES - 1, 0], tile[SLICES - 1, 1]
    freq = forward(tables, f_real * t_real - f_imag * t_imag, f_real * t_imag + f_imag * t_real)
    out = []
    for parity in range(2):
        real, imag = freq[parity][:, :CORE], freq[parity][:, CORE:]
        residue = real * real + imag * imag - patterns[:, pl.ds(parity * CORE, CORE)]
        out.append(beside(residue * real, residue * imag))
    u_real, u_imag = backward(tables, out)
    for layer in reversed(range(SLICES)):
        if layer > 0:
            f_real, f_imag = field[layer - 1, 0], field[layer - 1, 1]
        else:
            f_real, f_imag = lit[0], lit[1]
        real = f_real * u_real + f_imag * u_imag
        imag = f_real * u_imag - f_imag * u_real
        part_first[layer], part_second[layer] = pack(nearby, real[:, :CORE], imag[:, :CORE])
        send_far[layer], send_near[layer] = pack(nearby, real[:, CORE:], imag[:, CORE:])
        if layer > 0:
            t_real, t_imag = tile[layer, 0], tile[layer, 1]
            u_real, u_imag = propagate(
                tables,
                t_real * u_real + t_imag * u_imag,
                t_real * u_imag - t_imag * u_real,
                wave,
                -1,
            )


def call(body, outs, scratch=(), smem=0, count=0, limit=8):
    return pl.pallas_call(
        body,
        out_shape=[jax.ShapeDtypeStruct(shape, jnp.float32) for shape in outs],
        in_specs=[pl.BlockSpec(memory_space=pltpu.SMEM)] * smem
        + [pl.BlockSpec(memory_space=pltpu.VMEM)] * count,
        out_specs=[pl.BlockSpec(memory_space=pltpu.VMEM)] * len(outs),
        scratch_shapes=list(scratch),
        compiler_params=pltpu.CompilerParams(vmem_limit_bytes=limit << 20),
        name=body.__name__,
    )


PACK = (SLICES, TILE, CORE)
HALF = (SLICES, CORE, CORE)
RIMS = (2, SLICES, MARGIN, CORE)


def step(*args):
    return call(
        step_kernel,
        (PACK, PACK, PACK, PACK),
        (
            pltpu.VMEM((SLICES, 2, TILE, TILE), jnp.float32),
            pltpu.VMEM((SLICES - 1, 2, TILE, TILE), jnp.float32),
        ),
        count=8,
        limit=24,
    )(*args)


def three(value):
    high = value.astype(jnp.bfloat16)
    rest = value - high.astype(jnp.float32)
    middle = rest.astype(jnp.bfloat16)
    low = (rest - middle.astype(jnp.float32)).astype(jnp.bfloat16)
    return high, middle, low


def reorder(order, value):
    high, middle, low = three(value)
    rows = (dot(order[0], high) + dot(order[0], middle)) + dot(order[0], low)
    high, middle, low = three(rows)
    return (dot(high, order[1]) + dot(middle, order[1])) + dot(low, order[1])


def setup_kernel(positions, probe, phase, patterns, order, lit, ordered_phase, ordered_patterns):
    rows = lax.rem(positions[0] + (TILE - MARGIN), TILE)
    cols = lax.rem(positions[1] + (TILE - MARGIN), TILE)
    for part in range(2):
        lit[part] = pltpu.roll(pltpu.roll(probe[part], rows, 0), cols, 1)
    ordered_phase[...] = reorder(order, phase[...])
    ordered_patterns[...] = reorder(order, patterns[...])


def setup(positions, probe, phase, patterns, order):
    shapes = ((2, TILE, TILE), (TILE, TILE), (TILE, TILE))
    return call(setup_kernel, shapes, smem=1, count=4)(positions, probe, phase, patterns, order)


def open_kernel(core, first, second, near, far):
    even = even_row()
    nearby = near_lanes(CORE)
    for layer in range(SLICES):
        packs = pack(nearby, core[layer, 0], core[layer, 1])
        for k, (value, whole) in enumerate(zip(packs, (first, second))):
            whole[layer] = value
            near[k, layer] = jnp.where(even, value[MARGIN:], value[:MARGIN])
            far[k, layer] = jnp.where(even, value[:MARGIN], value[MARGIN:])


def begin(core):
    return call(open_kernel, (HALF, HALF, RIMS, RIMS), count=1)(core)


def assemble_kernel(core_1, core_2, near, far, first, second):
    even = even_row()
    for k, (core, mid) in enumerate(((core_1, first), (core_2, second))):
        for layer in range(SLICES):
            mid[layer, :CORE] = core[layer]
            mid[layer, CORE : CORE + MARGIN] = jnp.where(even, near[k, layer], far[k, layer])
            mid[layer, CORE + MARGIN :] = jnp.where(even, far[k, layer], near[k, layer])


def assemble(*args):
    return call(assemble_kernel, (PACK, PACK), count=4)(*args)


def share_kernel(part_1, part_2, came_1, came_2, total, send_near, send_far):
    even = even_row()
    for k, (part, came) in enumerate(((part_1, came_1), (part_2, came_2))):
        for layer in range(SLICES):
            value = part[layer] + came[layer]
            total[k, layer] = value
            a, b, d, e = (value[n * MARGIN : (n + 1) * MARGIN] for n in range(4))
            send_near[k, layer, :MARGIN] = jnp.where(even, b, e)
            send_near[k, layer, MARGIN:] = jnp.where(even, d, a)
            send_far[k, layer, :MARGIN] = jnp.where(even, e, b)
            send_far[k, layer, MARGIN:] = jnp.where(even, a, d)


def share(*args):
    return call(share_kernel, ((2, *PACK), (2, *HALF), (2, *HALF)), count=4)(*args)


def update_kernel(mid_1, mid_2, total, near, far, new_1, new_2):
    even = even_row()
    row = lax.axis_index("ty")
    above = jnp.where(row == 0, 0.0, STEP_SIZE)
    below = jnp.where(row == lax.axis_size("ty") - 1, 0.0, STEP_SIZE)
    for k, (mid, new) in enumerate(((mid_1, new_1), (mid_2, new_2))):
        for layer in range(SLICES):
            e, o = near[k, layer], far[k, layer]
            down = jnp.where(even, e, o)
            up = jnp.where(even, o, e)
            for n, (added, scale) in enumerate(
                (
                    (up[MARGIN:], STEP_SIZE),
                    (down[:MARGIN], STEP_SIZE),
                    (down[MARGIN:], below),
                    (up[:MARGIN], above),
                )
            ):
                rows = pl.ds(n * MARGIN, MARGIN)
                new[layer, rows] = mid[layer, rows] - scale * (total[k, layer, rows] + added)


def update(*args):
    return call(update_kernel, (PACK, PACK), count=5)(*args)


def close_kernel(part_1, part_2, came_1, came_2, total, send_near, send_far):
    even = even_row()
    for k, (part, came) in enumerate(((part_1, came_1), (part_2, came_2))):
        for layer in range(SLICES):
            value = part[layer] + came[layer]
            total[k, layer] = value[:CORE]
            below, above = value[CORE : CORE + MARGIN], value[CORE + MARGIN :]
            send_near[k, layer] = jnp.where(even, below, above)
            send_far[k, layer] = jnp.where(even, above, below)


def close(*args):
    return call(close_kernel, ((2, *HALF), RIMS, RIMS), count=4)(*args)


def finish_kernel(mid_1, mid_2, total, near, far, out):
    even = even_row()
    nearby = near_lanes(MARGIN)
    for layer in range(SLICES):
        for half in range(2):
            rows = pl.ds(half * MARGIN, MARGIN)
            packs = []
            for k, mid in enumerate((mid_1, mid_2)):
                e, o = near[k, layer], far[k, layer]
                added = jnp.where(even, o, e) if half == 0 else jnp.where(even, e, o)
                packs.append(mid[layer, rows] - STEP_SIZE * (total[k, layer, rows] + added))
            out[layer, 0, rows], out[layer, 1, rows] = unpack(nearby, *packs)


def finish(*args):
    return call(finish_kernel, ((SLICES, 2, CORE, CORE),), count=5)(*args)[0]


def swap(axis, first, block):
    count = lax.axis_size(axis)
    pairs = [(i, i + 1) for i in range(first, count - 1, 2)]
    return lax.ppermute(block, axis, pairs + [(j, i) for i, j in pairs])


def swap_rows(near, far):
    far = swap("ty", 1, far)
    return swap("ty", 0, near), far


def shards(object_field, probe, propagator_phase, patterns, scan_positions):
    first, second, near, far = begin(object_field)
    near, far = swap_rows(near, far)
    lit, phase, ordered = setup(
        scan_positions[0, 0, 0], probe, propagator_phase, patterns[0, 0, 0], order_table()
    )
    wave = jnp.stack([jnp.cos(phase), jnp.sin(phase)])
    tables = jnp.asarray(half_tables())
    first, second = assemble(first, second, near, far)
    for turn in range(STEPS):
        far = swap("tx", 1, second)
        near = swap("tx", 0, first)
        part_1, part_2, near, far = step(
            first, second, near, far, lit, wave, ordered, tables
        )
        far = swap("tx", 1, far)
        near = swap("tx", 0, near)
        if turn < STEPS - 1:
            total, near, far = share(part_1, part_2, near, far)
            near, far = swap_rows(near, far)
            first, second = update(first, second, total, near, far)
    total, near, far = close(part_1, part_2, near, far)
    near, far = swap_rows(near, far)
    return finish(first, second, total, near, far)


def solution(mesh):
    placed = (
        P(None, None, "ty", "tx"),
        P(),
        P(),
        P("ty", "tx", None, None, None),
        P("ty", "tx", None, None),
    )
    return jax.shard_map(
        shards, mesh=mesh, in_specs=placed, out_specs=P(None, None, "ty", "tx"), check_vma=False
    )
```

```python
import functools
import math

import jax
import jax.numpy as jnp
import numpy as np
from jax import lax
from jax.experimental import pallas as pl
from jax.experimental.pallas import tpu as pltpu
from jax.sharding import PartitionSpec as P

MARGIN = 64
CORE = 128
TILE = 256
SLICES = 3
STEPS = 2
STEP_SIZE = 0.05


def half_tables():
    index = np.arange(CORE)
    tables = []
    for parity in range(2):
        freq = 2 * index + parity
        angle = 2.0 * math.pi * ((freq[:, None] * index[None, :]) % TILE) / TILE
        real, imag = np.cos(angle) / 16.0, -np.sin(angle) / 16.0
        block = np.block([[real, -imag], [imag, real]]).astype(np.float32)
        for table in (block, block.T):
            high = table.astype(jnp.bfloat16)
            low = (table - high.astype(np.float32)).astype(jnp.bfloat16)
            tables.append(np.stack([high, low]))
    return np.stack(tables)


def order_table():
    table = np.zeros((TILE, TILE), np.float32)
    index = np.arange(CORE)
    table[index, 2 * index] = 1.0
    table[CORE + index, 2 * index + 1] = 1.0
    return np.stack([table, table.T]).astype(jnp.bfloat16)


def dot(left, right):
    return jnp.dot(left, right, preferred_element_type=jnp.float32)


def split(value):
    high = value.astype(jnp.bfloat16)
    low = (value - high.astype(jnp.float32)).astype(jnp.bfloat16)
    return high, low


def from_left(tables, which, value):
    high, low = split(value)
    both = dot(tables[which].reshape(2 * TILE, TILE), high)
    return both[:TILE] + (both[TILE:] + dot(tables[which, 0], low))


def from_right(tables, which, value):
    high, low = split(value)
    both = dot(jnp.concatenate([high, low], axis=0), tables[which, 0])
    return both[:TILE] + (both[TILE:] + dot(high, tables[which, 1]))


def stack(*rows):
    return jnp.concatenate(rows, axis=0)


def beside(*cols):
    return jnp.concatenate(cols, axis=1)


def forward(tables, real, imag):
    half = []
    for parity in range(2):
        if parity == 0:
            mixed = stack(real[:CORE] + real[CORE:], imag[:CORE] + imag[CORE:])
        else:
            mixed = stack(real[:CORE] - real[CORE:], imag[:CORE] - imag[CORE:])
        half.append(from_left(tables, 2 * parity, mixed))
    out = []
    for parity in range(2):
        rows = []
        for value in half:
            parts = []
            for part in (value[:CORE], value[CORE:]):
                first, second = part[:, :CORE], part[:, CORE:]
                parts.append(first + second if parity == 0 else first - second)
            rows.append(beside(*parts))
        out.append(from_right(tables, 2 * parity + 1, stack(*rows)))
    return out


def backward(tables, freq):
    even = from_right(tables, 0, freq[0])
    odd = from_right(tables, 2, freq[1])
    first, second = even + odd, even - odd
    half = []
    for parity in range(2):
        rows = slice(parity * CORE, (parity + 1) * CORE)
        mixed = stack(
            beside(first[rows, :CORE], second[rows, :CORE]),
            beside(first[rows, CORE:], second[rows, CORE:]),
        )
        half.append(from_left(tables, 2 * parity + 1, mixed))
    even, odd = half
    real = stack(even[:CORE] + odd[:CORE], even[:CORE] - odd[:CORE])
    imag = stack(even[CORE:] + odd[CORE:], even[CORE:] - odd[CORE:])
    return real, imag


def propagate(tables, real, imag, wave, sign):
    freq = forward(tables, real, imag)
    out = []
    for parity in range(2):
        real, imag = freq[parity][:, :CORE], freq[parity][:, CORE:]
        cols = pl.ds(parity * CORE, CORE)
        h_real, h_imag = wave[0, :, cols], wave[1, :, cols]
        if sign < 0:
            out.append(beside(real * h_real + imag * h_imag, imag * h_real - real * h_imag))
        else:
            out.append(beside(real * h_real - imag * h_imag, imag * h_real + real * h_imag))
    return backward(tables, out)


def even_row():
    return lax.rem(lax.axis_index("ty"), 2) == 0


def low_lanes(shape):
    return lax.broadcasted_iota(jnp.int32, shape, len(shape) - 1) < MARGIN


def turned(value):
    return pltpu.roll(value, MARGIN, 1)


def near_lanes(rows):
    return low_lanes((rows, CORE)) != (lax.rem(lax.axis_index("tx"), 2) == 0)


def pack(nearby, real, imag):
    other = turned(imag)
    return jnp.where(nearby, real, other), jnp.where(nearby, other, real)


def unpack(nearby, first, second):
    return jnp.where(nearby, first, second), turned(jnp.where(nearby, second, first))


def rows_of(refs, layer):
    return stack(*(ref[layer] for ref in refs))


def put_rows(refs, layer, value):
    if len(refs) == 1:
        refs[0][layer] = value
    else:
        refs[0][layer] = value[:CORE]
        refs[1][layer] = value[CORE:]


def step_kernel(blocks, cuts, *refs):
    taken = [refs[k * blocks : (k + 1) * blocks] for k in range(4)]
    first, second, near, far = taken
    lit, wave, patterns, tables, part_first, part_second = refs[4 * blocks : 4 * blocks + 6]
    sends = refs[4 * blocks + 6 : -2]
    send_near, send_far = sends[:cuts], sends[cuts:]
    tile, field = refs[-2:]
    nearby = near_lanes(TILE)
    for layer in range(SLICES):
        core = unpack(nearby, rows_of(first, layer), rows_of(second, layer))
        margin = unpack(nearby, rows_of(far, layer), rows_of(near, layer))
        for c in range(2):
            tile[layer, c] = beside(core[c], margin[c])
    f_real, f_imag = lit[0], lit[1]
    for layer in range(SLICES - 1):
        t_real, t_imag = tile[layer, 0], tile[layer, 1]
        f_real, f_imag = propagate(
            tables, f_real * t_real - f_imag * t_imag, f_real * t_imag + f_imag * t_real, wave, 1
        )
        field[layer, 0] = f_real
        field[layer, 1] = f_imag
    t_real, t_imag = tile[SLICES - 1, 0], tile[SLICES - 1, 1]
    freq = forward(tables, f_real * t_real - f_imag * t_imag, f_real * t_imag + f_imag * t_real)
    out = []
    for parity in range(2):
        real, imag = freq[parity][:, :CORE], freq[parity][:, CORE:]
        residue = real * real + imag * imag - patterns[:, pl.ds(parity * CORE, CORE)]
        out.append(beside(residue * real, residue * imag))
    u_real, u_imag = backward(tables, out)
    for layer in reversed(range(SLICES)):
        if layer > 0:
            f_real, f_imag = field[layer - 1, 0], field[layer - 1, 1]
        else:
            f_real, f_imag = lit[0], lit[1]
        real = f_real * u_real + f_imag * u_imag
        imag = f_real * u_imag - f_imag * u_real
        part_first[layer], part_second[layer] = pack(nearby, real[:, :CORE], imag[:, :CORE])
        far_pack, near_pack = pack(nearby, real[:, CORE:], imag[:, CORE:])
        put_rows(send_far, layer, far_pack)
        put_rows(send_near, layer, near_pack)
        if layer > 0:
            t_real, t_imag = tile[layer, 0], tile[layer, 1]
            u_real, u_imag = propagate(
                tables,
                t_real * u_real + t_imag * u_imag,
                t_real * u_imag - t_imag * u_real,
                wave,
                -1,
            )


def call(body, outs, scratch=(), smem=0, count=0, limit=8, name=None):
    return pl.pallas_call(
        body,
        out_shape=[jax.ShapeDtypeStruct(shape, jnp.float32) for shape in outs],
        in_specs=[pl.BlockSpec(memory_space=pltpu.SMEM)] * smem
        + [pl.BlockSpec(memory_space=pltpu.VMEM)] * count,
        out_specs=[pl.BlockSpec(memory_space=pltpu.VMEM)] * len(outs),
        scratch_shapes=list(scratch),
        compiler_params=pltpu.CompilerParams(vmem_limit_bytes=limit << 20),
        name=name or body.__name__,
    )


PACK = (SLICES, TILE, CORE)
HALF = (SLICES, CORE, CORE)
RIMS = (2, SLICES, MARGIN, CORE)


def step(blocks, cuts, *args):
    out = call(
        functools.partial(step_kernel, blocks, cuts),
        (PACK, PACK) + ((PACK,) * 2 if cuts == 1 else (HALF,) * 4),
        (
            pltpu.VMEM((SLICES, 2, TILE, TILE), jnp.float32),
            pltpu.VMEM((SLICES - 1, 2, TILE, TILE), jnp.float32),
        ),
        count=4 * blocks + 4,
        limit=24,
        name="step_kernel",
    )(*args)
    return out[:2], out[2 : 2 + cuts], out[2 + cuts :]


def three(value):
    high = value.astype(jnp.bfloat16)
    rest = value - high.astype(jnp.float32)
    middle = rest.astype(jnp.bfloat16)
    low = (rest - middle.astype(jnp.float32)).astype(jnp.bfloat16)
    return high, middle, low


def reorder(order, value):
    high, middle, low = three(value)
    rows = (dot(order[0], high) + dot(order[0], middle)) + dot(order[0], low)
    high, middle, low = three(rows)
    return (dot(high, order[1]) + dot(middle, order[1])) + dot(low, order[1])


def setup_kernel(positions, probe, phase, patterns, order, lit, ordered_phase, ordered_patterns):
    rows = lax.rem(positions[0] + (TILE - MARGIN), TILE)
    cols = lax.rem(positions[1] + (TILE - MARGIN), TILE)
    for part in range(2):
        lit[part] = pltpu.roll(pltpu.roll(probe[part], rows, 0), cols, 1)
    ordered_phase[...] = reorder(order, phase[...])
    ordered_patterns[...] = reorder(order, patterns[...])


def setup(positions, probe, phase, patterns, order):
    shapes = ((2, TILE, TILE), (TILE, TILE), (TILE, TILE))
    return call(setup_kernel, shapes, smem=1, count=4)(positions, probe, phase, patterns, order)


def open_kernel(core, first, second, near, far):
    even = even_row()
    nearby = near_lanes(CORE)
    for layer in range(SLICES):
        packs = pack(nearby, core[layer, 0], core[layer, 1])
        for k, (value, whole) in enumerate(zip(packs, (first, second))):
            whole[layer] = value
            near[k, layer] = jnp.where(even, value[MARGIN:], value[:MARGIN])
            far[k, layer] = jnp.where(even, value[:MARGIN], value[MARGIN:])


def begin(core):
    return call(open_kernel, (HALF, HALF, RIMS, RIMS), count=1)(core)


def margin_kernel(near, far, first, second):
    even = even_row()
    for k, margin in enumerate((first, second)):
        for layer in range(SLICES):
            margin[layer, :MARGIN] = jnp.where(even, near[k, layer], far[k, layer])
            margin[layer, MARGIN:] = jnp.where(even, far[k, layer], near[k, layer])


def margins(*args):
    return call(margin_kernel, (HALF, HALF), count=2)(*args)


def share_kernel(part_1, part_2, came_1, came_2, total, send_near, send_far):
    even = even_row()
    for k, (part, came) in enumerate(((part_1, came_1), (part_2, came_2))):
        for layer in range(SLICES):
            value = part[layer] + came[layer]
            total[k, layer] = value
            a, b, d, e = (value[n * MARGIN : (n + 1) * MARGIN] for n in range(4))
            send_near[k, layer, :MARGIN] = jnp.where(even, b, e)
            send_near[k, layer, MARGIN:] = jnp.where(even, d, a)
            send_far[k, layer, :MARGIN] = jnp.where(even, e, b)
            send_far[k, layer, MARGIN:] = jnp.where(even, a, d)


def share(*args):
    return call(share_kernel, ((2, *PACK), (2, *HALF), (2, *HALF)), count=4)(*args)


def update_kernel(core_1, core_2, margin_1, margin_2, total, near, far, new_1, new_2):
    even = even_row()
    row = lax.axis_index("ty")
    above = jnp.where(row == 0, 0.0, STEP_SIZE)
    below = jnp.where(row == lax.axis_size("ty") - 1, 0.0, STEP_SIZE)
    for k, (mid, new) in enumerate((((core_1, margin_1), new_1), ((core_2, margin_2), new_2))):
        for layer in range(SLICES):
            e, o = near[k, layer], far[k, layer]
            down = jnp.where(even, e, o)
            up = jnp.where(even, o, e)
            for n, (added, scale) in enumerate(
                (
                    (up[MARGIN:], STEP_SIZE),
                    (down[:MARGIN], STEP_SIZE),
                    (down[MARGIN:], below),
                    (up[:MARGIN], above),
                )
            ):
                rows = pl.ds(n * MARGIN, MARGIN)
                old = mid[n // 2][layer, pl.ds(n % 2 * MARGIN, MARGIN)]
                new[layer, rows] = old - scale * (total[k, layer, rows] + added)


def update(*args):
    return call(update_kernel, (PACK, PACK), count=7)(*args)


def close_kernel(part_1, part_2, came_1, came_2, send_near, send_far):
    even = even_row()
    for k, (part, came) in enumerate(((part_1, came_1), (part_2, came_2))):
        for layer in range(SLICES):
            value = part[layer, CORE:] + came[layer]
            below, above = value[:MARGIN], value[MARGIN:]
            send_near[k, layer] = jnp.where(even, below, above)
            send_far[k, layer] = jnp.where(even, above, below)


def close(*args):
    return call(close_kernel, (RIMS, RIMS), count=4)(*args)


def finish_kernel(mid_1, mid_2, part_1, part_2, came_1, came_2, near, far, out):
    even = even_row()
    nearby = near_lanes(MARGIN)
    for layer in range(SLICES):
        for half in range(2):
            rows = pl.ds(half * MARGIN, MARGIN)
            packs = []
            for k, (mid, part, came) in enumerate(
                ((mid_1, part_1, came_1), (mid_2, part_2, came_2))
            ):
                e, o = near[k, layer], far[k, layer]
                added = jnp.where(even, o, e) if half == 0 else jnp.where(even, e, o)
                total = part[layer, rows] + came[layer, rows]
                packs.append(mid[layer, rows] - STEP_SIZE * (total + added))
            out[layer, 0, rows], out[layer, 1, rows] = unpack(nearby, *packs)


def finish(*args):
    return call(finish_kernel, ((SLICES, 2, CORE, CORE),), count=8)(*args)[0]


def swap(axis, first, block):
    count = lax.axis_size(axis)
    pairs = [(i, i + 1) for i in range(first, count - 1, 2)]
    return lax.ppermute(block, axis, pairs + [(j, i) for i, j in pairs])


def swap_rows(near, far):
    far = swap("ty", 1, far)
    return swap("ty", 0, near), far


def swap_cols(near, far):
    far = swap("tx", 1, far)
    near = swap("tx", 0, near)
    return near, far


def shards(object_field, probe, propagator_phase, patterns, scan_positions):
    first, second, near, far = begin(object_field)
    near, far = swap_rows(near, far)
    core_near, core_far = swap_cols(first, second)
    lit, phase, ordered = setup(
        scan_positions[0, 0, 0], probe, propagator_phase, patterns[0, 0, 0], order_table()
    )
    wave = jnp.stack([jnp.cos(phase), jnp.sin(phase)])
    tables = jnp.asarray(half_tables())
    shared = (lit, wave, ordered, tables)
    margin_1, margin_2 = margins(near, far)
    rim_near, rim_far = swap_cols(margin_1, margin_2)
    taken = (first, margin_1, second, margin_2, core_near, rim_near, core_far, rim_far)
    parts, (near,), (far,) = step(2, 1, *taken, *shared)

    near, far = swap_cols(near, far)
    total, near, far = share(*parts, near, far)
    near, far = swap_rows(near, far)
    first, second = update(first, second, margin_1, margin_2, total, near, far)
    near, far = swap_cols(first, second)
    parts, near, far = step(1, 2, first, second, near, far, *shared)

    rim_near, rim_far = swap_cols(near[1], far[1])
    core_near, core_far = swap_cols(near[0], far[0])
    near, far = swap_rows(*close(*parts, rim_near, rim_far))
    return finish(first, second, *parts, core_near, core_far, near, far)


def solution(mesh):
    placed = (
        P(None, None, "ty", "tx"),
        P(),
        P(),
        P("ty", "tx", None, None, None),
        P("ty", "tx", None, None),
    )
    return jax.shard_map(
        shards, mesh=mesh, in_specs=placed, out_specs=P(None, None, "ty", "tx"), check_vma=False
    )
```

```python
import functools
import math

import jax
import jax.numpy as jnp
import numpy as np
from jax import lax
from jax.experimental import pallas as pl
from jax.experimental.pallas import tpu as pltpu
from jax.sharding import PartitionSpec as P

MARGIN = 64
CORE = 128
TILE = 256
SLICES = 3
STEPS = 2
STEP_SIZE = 0.05


def half_tables():
    index = np.arange(CORE)
    tables = []
    for parity in range(2):
        freq = 2 * index + parity
        angle = 2.0 * math.pi * ((freq[:, None] * index[None, :]) % TILE) / TILE
        real, imag = np.cos(angle) / 16.0, -np.sin(angle) / 16.0
        block = np.block([[real, -imag], [imag, real]]).astype(np.float32)
        for table in (block, block.T):
            high = table.astype(jnp.bfloat16)
            low = (table - high.astype(np.float32)).astype(jnp.bfloat16)
            tables.append(np.stack([high, low]))
    return np.stack(tables)


def order_table():
    table = np.zeros((TILE, TILE), np.float32)
    index = np.arange(CORE)
    table[index, 2 * index] = 1.0
    table[CORE + index, 2 * index + 1] = 1.0
    return np.stack([table, table.T]).astype(jnp.bfloat16)


def dot(left, right):
    return jnp.dot(left, right, preferred_element_type=jnp.float32)


def split(value):
    high = value.astype(jnp.bfloat16)
    low = (value - high.astype(jnp.float32)).astype(jnp.bfloat16)
    return high, low


def from_left(tables, which, value):
    high, low = split(value)
    both = dot(tables[which].reshape(2 * TILE, TILE), high)
    return both[:TILE] + (both[TILE:] + dot(tables[which, 0], low))


def from_right(tables, which, value):
    high, low = split(value)
    both = dot(jnp.concatenate([high, low], axis=0), tables[which, 0])
    return both[:TILE] + (both[TILE:] + dot(high, tables[which, 1]))


def stack(*rows):
    return jnp.concatenate(rows, axis=0)


def beside(*cols):
    return jnp.concatenate(cols, axis=1)


def forward(tables, real, imag):
    half = []
    for parity in range(2):
        if parity == 0:
            mixed = stack(real[:CORE] + real[CORE:], imag[:CORE] + imag[CORE:])
        else:
            mixed = stack(real[:CORE] - real[CORE:], imag[:CORE] - imag[CORE:])
        half.append(from_left(tables, 2 * parity, mixed))
    out = []
    for parity in range(2):
        rows = []
        for value in half:
            parts = []
            for part in (value[:CORE], value[CORE:]):
                first, second = part[:, :CORE], part[:, CORE:]
                parts.append(first + second if parity == 0 else first - second)
            rows.append(beside(*parts))
        out.append(from_right(tables, 2 * parity + 1, stack(*rows)))
    return out


def backward(tables, freq):
    even = from_right(tables, 0, freq[0])
    odd = from_right(tables, 2, freq[1])
    first, second = even + odd, even - odd
    half = []
    for parity in range(2):
        rows = slice(parity * CORE, (parity + 1) * CORE)
        mixed = stack(
            beside(first[rows, :CORE], second[rows, :CORE]),
            beside(first[rows, CORE:], second[rows, CORE:]),
        )
        half.append(from_left(tables, 2 * parity + 1, mixed))
    even, odd = half
    real = stack(even[:CORE] + odd[:CORE], even[:CORE] - odd[:CORE])
    imag = stack(even[CORE:] + odd[CORE:], even[CORE:] - odd[CORE:])
    return real, imag


def propagate(tables, real, imag, wave, sign):
    freq = forward(tables, real, imag)
    out = []
    for parity in range(2):
        real, imag = freq[parity][:, :CORE], freq[parity][:, CORE:]
        cols = pl.ds(parity * CORE, CORE)
        h_real, h_imag = wave[0, :, cols], wave[1, :, cols]
        if sign < 0:
            out.append(beside(real * h_real + imag * h_imag, imag * h_real - real * h_imag))
        else:
            out.append(beside(real * h_real - imag * h_imag, imag * h_real + real * h_imag))
    return backward(tables, out)


def even_row():
    return lax.rem(lax.axis_index("ty"), 2) == 0


def low_lanes(shape):
    return lax.broadcasted_iota(jnp.int32, shape, len(shape) - 1) < MARGIN


def turned(value):
    return pltpu.roll(value, MARGIN, 1)


def near_lanes(rows):
    return low_lanes((rows, CORE)) != (lax.rem(lax.axis_index("tx"), 2) == 0)


def pack(nearby, real, imag):
    other = turned(imag)
    return jnp.where(nearby, real, other), jnp.where(nearby, other, real)


def unpack(nearby, first, second):
    return jnp.where(nearby, first, second), turned(jnp.where(nearby, second, first))


def step_kernel(
    first,
    second,
    near,
    far,
    lit,
    wave,
    patterns,
    tables,
    part_first,
    part_second,
    send_near,
    send_far,
    tile,
    field,
):
    nearby = near_lanes(TILE)

    for layer in range(SLICES):
        core = unpack(nearby, first[layer], second[layer])
        margin = unpack(nearby, far[layer], near[layer])
        for c in range(2):
            tile[layer, c] = beside(core[c], margin[c])
    f_real, f_imag = lit[0], lit[1]
    for layer in range(SLICES - 1):
        t_real, t_imag = tile[layer, 0], tile[layer, 1]
        f_real, f_imag = propagate(
            tables, f_real * t_real - f_imag * t_imag, f_real * t_imag + f_imag * t_real, wave, 1
        )
        field[layer, 0] = f_real
        field[layer, 1] = f_imag
    t_real, t_imag = tile[SLICES - 1, 0], tile[SLICES - 1, 1]
    freq = forward(tables, f_real * t_real - f_imag * t_imag, f_real * t_imag + f_imag * t_real)
    out = []
    for parity in range(2):
        real, imag = freq[parity][:, :CORE], freq[parity][:, CORE:]
        residue = real * real + imag * imag - patterns[:, pl.ds(parity * CORE, CORE)]
        out.append(beside(residue * real, residue * imag))
    u_real, u_imag = backward(tables, out)
    for layer in reversed(range(SLICES)):
        if layer > 0:
            f_real, f_imag = field[layer - 1, 0], field[layer - 1, 1]
        else:
            f_real, f_imag = lit[0], lit[1]
        real = f_real * u_real + f_imag * u_imag
        imag = f_real * u_imag - f_imag * u_real
        part_first[layer], part_second[layer] = pack(nearby, real[:, :CORE], imag[:, :CORE])
        send_far[layer], send_near[layer] = pack(nearby, real[:, CORE:], imag[:, CORE:])
        if layer > 0:
            t_real, t_imag = tile[layer, 0], tile[layer, 1]
            u_real, u_imag = propagate(
                tables,
                t_real * u_real + t_imag * u_imag,
                t_real * u_imag - t_imag * u_real,
                wave,
                -1,
            )


def call(body, outs, scratch=(), smem=0, count=0, limit=8):
    return pl.pallas_call(
        body,
        out_shape=[jax.ShapeDtypeStruct(shape, jnp.float32) for shape in outs],
        in_specs=[pl.BlockSpec(memory_space=pltpu.SMEM)] * smem
        + [pl.BlockSpec(memory_space=pltpu.VMEM)] * count,
        out_specs=[pl.BlockSpec(memory_space=pltpu.VMEM)] * len(outs),
        scratch_shapes=list(scratch),
        compiler_params=pltpu.CompilerParams(vmem_limit_bytes=limit << 20),
        name=body.__name__,
    )


PACK = (SLICES, TILE, CORE)
HALF = (SLICES, CORE, CORE)
RIMS = (2, SLICES, MARGIN, CORE)


def step(*args):
    return call(
        step_kernel,
        (PACK, PACK, PACK, PACK),
        (
            pltpu.VMEM((SLICES, 2, TILE, TILE), jnp.float32),
            pltpu.VMEM((SLICES - 1, 2, TILE, TILE), jnp.float32),
        ),
        count=8,
        limit=24,
    )(*args)


def three(value):
    high = value.astype(jnp.bfloat16)
    rest = value - high.astype(jnp.float32)
    middle = rest.astype(jnp.bfloat16)
    low = (rest - middle.astype(jnp.float32)).astype(jnp.bfloat16)
    return high, middle, low


def reorder(order, value):
    high, middle, low = three(value)
    rows = (dot(order[0], high) + dot(order[0], middle)) + dot(order[0], low)
    high, middle, low = three(rows)
    return (dot(high, order[1]) + dot(middle, order[1])) + dot(low, order[1])


def setup_kernel(positions, probe, phase, patterns, order, lit, ordered_phase, ordered_patterns):
    rows = lax.rem(positions[0] + (TILE - MARGIN), TILE)
    cols = lax.rem(positions[1] + (TILE - MARGIN), TILE)
    for part in range(2):
        lit[part] = pltpu.roll(pltpu.roll(probe[part], rows, 0), cols, 1)
    ordered_phase[...] = reorder(order, phase[...])
    ordered_patterns[...] = reorder(order, patterns[...])


def setup(positions, probe, phase, patterns, order):
    shapes = ((2, TILE, TILE), (TILE, TILE), (TILE, TILE))
    return call(setup_kernel, shapes, smem=1, count=4)(positions, probe, phase, patterns, order)


def planes(source, target, sems):
    return [
        pltpu.make_async_copy(source.at[layer, c], target.at[layer, c], sems.at[layer, c])
        for layer in range(SLICES)
        for c in range(2)
    ]


def open_kernel(whole, first, second, near, far, core, sems):
    copies = planes(whole, core, sems)
    for copy in copies:
        copy.start()
    even = even_row()
    nearby = near_lanes(CORE)
    for layer in range(SLICES):
        copies[2 * layer].wait()
        copies[2 * layer + 1].wait()
        packs = pack(nearby, core[layer, 0], core[layer, 1])
        for k, (value, kept) in enumerate(zip(packs, (first, second))):
            kept[layer] = value
            near[k, layer] = jnp.where(even, value[MARGIN:], value[:MARGIN])
            far[k, layer] = jnp.where(even, value[:MARGIN], value[MARGIN:])


BLOCK = (SLICES, 2, CORE, CORE)
COPIES = (pltpu.VMEM(BLOCK, jnp.float32), pltpu.SemaphoreType.DMA((SLICES, 2)))


def begin(core):
    return pl.pallas_call(
        open_kernel,
        out_shape=[jax.ShapeDtypeStruct(s, jnp.float32) for s in (HALF, HALF, RIMS, RIMS)],
        in_specs=[pl.BlockSpec(memory_space=pltpu.HBM)],
        out_specs=[pl.BlockSpec(memory_space=pltpu.VMEM)] * 4,
        scratch_shapes=list(COPIES),
        compiler_params=pltpu.CompilerParams(vmem_limit_bytes=8 << 20),
        name="open_kernel",
    )(pltpu.with_memory_space_constraint(core, pltpu.HBM))


def assemble_kernel(core_1, core_2, near, far, first, second):
    even = even_row()
    for k, (core, mid) in enumerate(((core_1, first), (core_2, second))):
        for layer in range(SLICES):
            mid[layer, :CORE] = core[layer]
            mid[layer, CORE : CORE + MARGIN] = jnp.where(even, near[k, layer], far[k, layer])
            mid[layer, CORE + MARGIN :] = jnp.where(even, far[k, layer], near[k, layer])


def assemble(*args):
    return call(assemble_kernel, (PACK, PACK), count=4)(*args)


def share_kernel(part_1, part_2, came_1, came_2, total, send_near, send_far):
    even = even_row()
    for k, (part, came) in enumerate(((part_1, came_1), (part_2, came_2))):
        for layer in range(SLICES):
            value = part[layer] + came[layer]
            total[k, layer] = value
            a, b, d, e = (value[n * MARGIN : (n + 1) * MARGIN] for n in range(4))
            send_near[k, layer, :MARGIN] = jnp.where(even, b, e)
            send_near[k, layer, MARGIN:] = jnp.where(even, d, a)
            send_far[k, layer, :MARGIN] = jnp.where(even, e, b)
            send_far[k, layer, MARGIN:] = jnp.where(even, a, d)


def share(*args):
    return call(share_kernel, ((2, *PACK), (2, *HALF), (2, *HALF)), count=4)(*args)


def update_kernel(mid_1, mid_2, total, near, far, new_1, new_2):
    even = even_row()
    row = lax.axis_index("ty")
    above = jnp.where(row == 0, 0.0, STEP_SIZE)
    below = jnp.where(row == lax.axis_size("ty") - 1, 0.0, STEP_SIZE)
    for k, (mid, new) in enumerate(((mid_1, new_1), (mid_2, new_2))):
        for layer in range(SLICES):
            e, o = near[k, layer], far[k, layer]
            down = jnp.where(even, e, o)
            up = jnp.where(even, o, e)
            for n, (added, scale) in enumerate(
                (
                    (up[MARGIN:], STEP_SIZE),
                    (down[:MARGIN], STEP_SIZE),
                    (down[MARGIN:], below),
                    (up[:MARGIN], above),
                )
            ):
                rows = pl.ds(n * MARGIN, MARGIN)
                new[layer, rows] = mid[layer, rows] - scale * (total[k, layer, rows] + added)


def update(*args):
    return call(update_kernel, (PACK, PACK), count=5)(*args)


def close_kernel(part_1, part_2, came_1, came_2, total, send_near, send_far):
    even = even_row()
    for k, (part, came) in enumerate(((part_1, came_1), (part_2, came_2))):
        for layer in range(SLICES):
            value = part[layer] + came[layer]
            total[k, layer] = value[:CORE]
            below, above = value[CORE : CORE + MARGIN], value[CORE + MARGIN :]
            send_near[k, layer] = jnp.where(even, below, above)
            send_far[k, layer] = jnp.where(even, above, below)


def close(*args):
    return call(close_kernel, ((2, *HALF), RIMS, RIMS), count=4)(*args)


def finish_kernel(mid_1, mid_2, total, near, far, whole, out, sems):
    copies = planes(out, whole, sems)
    even = even_row()
    nearby = near_lanes(MARGIN)
    for layer in range(SLICES):
        for half in range(2):
            rows = pl.ds(half * MARGIN, MARGIN)
            packs = []
            for k, mid in enumerate((mid_1, mid_2)):
                e, o = near[k, layer], far[k, layer]
                added = jnp.where(even, o, e) if half == 0 else jnp.where(even, e, o)
                packs.append(mid[layer, rows] - STEP_SIZE * (total[k, layer, rows] + added))
            out[layer, 0, rows], out[layer, 1, rows] = unpack(nearby, *packs)
        copies[2 * layer].start()
        copies[2 * layer + 1].start()
    for copy in copies:
        copy.wait()


def finish(*args):
    return pl.pallas_call(
        finish_kernel,
        out_shape=jax.ShapeDtypeStruct(BLOCK, jnp.float32),
        in_specs=[pl.BlockSpec(memory_space=pltpu.VMEM)] * 5,
        out_specs=pl.BlockSpec(memory_space=pltpu.HBM),
        scratch_shapes=list(COPIES),
        compiler_params=pltpu.CompilerParams(vmem_limit_bytes=8 << 20),
        name="finish_kernel",
    )(*args)


def swap(axis, first, block):
    count = lax.axis_size(axis)
    pairs = [(i, i + 1) for i in range(first, count - 1, 2)]
    return lax.ppermute(block, axis, pairs + [(j, i) for i, j in pairs])


def swap_rows(near, far):
    far = swap("ty", 1, far)
    return swap("ty", 0, near), far


def shards(object_field, probe, propagator_phase, patterns, scan_positions):
    first, second, near, far = begin(object_field)
    near, far = swap_rows(near, far)
    lit, phase, ordered = setup(
        scan_positions[0, 0, 0], probe, propagator_phase, patterns[0, 0, 0], order_table()
    )
    wave = jnp.stack([jnp.cos(phase), jnp.sin(phase)])
    tables = jnp.asarray(half_tables())
    first, second = assemble(first, second, near, far)
    for turn in range(STEPS):
        far = swap("tx", 1, second)
        near = swap("tx", 0, first)
        part_1, part_2, near, far = step(
            first, second, near, far, lit, wave, ordered, tables
        )
        far = swap("tx", 1, far)
        near = swap("tx", 0, near)
        if turn < STEPS - 1:
            total, near, far = share(part_1, part_2, near, far)
            near, far = swap_rows(near, far)
            first, second = update(first, second, total, near, far)
    total, near, far = close(part_1, part_2, near, far)
    near, far = swap_rows(near, far)
    return finish(first, second, total, near, far)


def solution(mesh):
    placed = (
        P(None, None, "ty", "tx"),
        P(),
        P(),
        P("ty", "tx", None, None, None),
        P("ty", "tx", None, None),
    )
    return jax.shard_map(
        shards, mesh=mesh, in_specs=placed, out_specs=P(None, None, "ty", "tx"), check_vma=False
    )
```

```python
import functools
import math

import jax
import jax.numpy as jnp
import numpy as np
from jax import lax
from jax.experimental import pallas as pl
from jax.experimental.pallas import tpu as pltpu
from jax.sharding import PartitionSpec as P

MARGIN = 64
CORE = 128
TILE = 256
SLICES = 3
STEPS = 2
STEP_SIZE = 0.05


def half_tables():
    index = np.arange(CORE)
    tables = []
    for parity in range(2):
        freq = 2 * index + parity
        angle = 2.0 * math.pi * ((freq[:, None] * index[None, :]) % TILE) / TILE
        real, imag = np.cos(angle) / 16.0, -np.sin(angle) / 16.0
        block = np.block([[real, -imag], [imag, real]]).astype(np.float32)
        for table in (block, block.T):
            high = table.astype(jnp.bfloat16)
            low = (table - high.astype(np.float32)).astype(jnp.bfloat16)
            tables.append(np.stack([high, low]))
    return np.stack(tables)


def order_table():
    table = np.zeros((TILE, TILE), np.float32)
    index = np.arange(CORE)
    table[index, 2 * index] = 1.0
    table[CORE + index, 2 * index + 1] = 1.0
    return np.stack([table, table.T]).astype(jnp.bfloat16)


def dot(left, right):
    return jnp.dot(left, right, preferred_element_type=jnp.float32)


def split(value):
    high = value.astype(jnp.bfloat16)
    low = (value - high.astype(jnp.float32)).astype(jnp.bfloat16)
    return high, low


def from_left(tables, which, value):
    high, low = split(value)
    both = dot(tables[which].reshape(2 * TILE, TILE), high)
    return both[:TILE] + (both[TILE:] + dot(tables[which, 0], low))


def from_right(tables, which, value):
    high, low = split(value)
    both = dot(jnp.concatenate([high, low], axis=0), tables[which, 0])
    return both[:TILE] + (both[TILE:] + dot(high, tables[which, 1]))


def stack(*rows):
    return jnp.concatenate(rows, axis=0)


def beside(*cols):
    return jnp.concatenate(cols, axis=1)


def forward(tables, real, imag):
    half = []
    for parity in range(2):
        if parity == 0:
            mixed = stack(real[:CORE] + real[CORE:], imag[:CORE] + imag[CORE:])
        else:
            mixed = stack(real[:CORE] - real[CORE:], imag[:CORE] - imag[CORE:])
        half.append(from_left(tables, 2 * parity, mixed))
    out = []
    for parity in range(2):
        rows = []
        for value in half:
            parts = []
            for part in (value[:CORE], value[CORE:]):
                first, second = part[:, :CORE], part[:, CORE:]
                parts.append(first + second if parity == 0 else first - second)
            rows.append(beside(*parts))
        out.append(from_right(tables, 2 * parity + 1, stack(*rows)))
    return out


def backward(tables, freq):
    even = from_right(tables, 0, freq[0])
    odd = from_right(tables, 2, freq[1])
    first, second = even + odd, even - odd
    half = []
    for parity in range(2):
        rows = slice(parity * CORE, (parity + 1) * CORE)
        mixed = stack(
            beside(first[rows, :CORE], second[rows, :CORE]),
            beside(first[rows, CORE:], second[rows, CORE:]),
        )
        half.append(from_left(tables, 2 * parity + 1, mixed))
    even, odd = half
    real = stack(even[:CORE] + odd[:CORE], even[:CORE] - odd[:CORE])
    imag = stack(even[CORE:] + odd[CORE:], even[CORE:] - odd[CORE:])
    return real, imag


def propagate(tables, real, imag, wave, sign):
    freq = forward(tables, real, imag)
    out = []
    for parity in range(2):
        real, imag = freq[parity][:, :CORE], freq[parity][:, CORE:]
        cols = pl.ds(parity * CORE, CORE)
        h_real, h_imag = wave[0, :, cols], wave[1, :, cols]
        if sign < 0:
            out.append(beside(real * h_real + imag * h_imag, imag * h_real - real * h_imag))
        else:
            out.append(beside(real * h_real - imag * h_imag, imag * h_real + real * h_imag))
    return backward(tables, out)


def even_row():
    return lax.rem(lax.axis_index("ty"), 2) == 0


def low_lanes(shape):
    return lax.broadcasted_iota(jnp.int32, shape, len(shape) - 1) < MARGIN


def turned(value):
    return pltpu.roll(value, MARGIN, 1)


def near_lanes(rows):
    return low_lanes((rows, CORE)) != (lax.rem(lax.axis_index("tx"), 2) == 0)


def pack(nearby, real, imag):
    other = turned(imag)
    return jnp.where(nearby, real, other), jnp.where(nearby, other, real)


def unpack(nearby, first, second):
    return jnp.where(nearby, first, second), turned(jnp.where(nearby, second, first))


def rows_of(refs, layer):
    return stack(*(ref[layer] for ref in refs))


def put_rows(refs, layer, value):
    if len(refs) == 1:
        refs[0][layer] = value
    else:
        refs[0][layer] = value[:CORE]
        refs[1][layer] = value[CORE:]


def step_kernel(blocks, cuts, *refs):
    taken = [refs[k * blocks : (k + 1) * blocks] for k in range(4)]
    first, second, near, far = taken
    lit, wave, patterns, tables, part_first, part_second = refs[4 * blocks : 4 * blocks + 6]
    sends = refs[4 * blocks + 6 : -2]
    send_near, send_far = sends[:cuts], sends[cuts:]
    tile, field = refs[-2:]
    nearby = near_lanes(TILE)
    for layer in range(SLICES):
        core = unpack(nearby, rows_of(first, layer), rows_of(second, layer))
        margin = unpack(nearby, rows_of(far, layer), rows_of(near, layer))
        for c in range(2):
            tile[layer, c] = beside(core[c], margin[c])
    f_real, f_imag = lit[0], lit[1]
    for layer in range(SLICES - 1):
        t_real, t_imag = tile[layer, 0], tile[layer, 1]
        f_real, f_imag = propagate(
            tables, f_real * t_real - f_imag * t_imag, f_real * t_imag + f_imag * t_real, wave, 1
        )
        field[layer, 0] = f_real
        field[layer, 1] = f_imag
    t_real, t_imag = tile[SLICES - 1, 0], tile[SLICES - 1, 1]
    freq = forward(tables, f_real * t_real - f_imag * t_imag, f_real * t_imag + f_imag * t_real)
    out = []
    for parity in range(2):
        real, imag = freq[parity][:, :CORE], freq[parity][:, CORE:]
        residue = real * real + imag * imag - patterns[:, pl.ds(parity * CORE, CORE)]
        out.append(beside(residue * real, residue * imag))
    u_real, u_imag = backward(tables, out)
    for layer in reversed(range(SLICES)):
        if layer > 0:
            f_real, f_imag = field[layer - 1, 0], field[layer - 1, 1]
        else:
            f_real, f_imag = lit[0], lit[1]
        real = f_real * u_real + f_imag * u_imag
        imag = f_real * u_imag - f_imag * u_real
        part_first[layer], part_second[layer] = pack(nearby, real[:, :CORE], imag[:, :CORE])
        far_pack, near_pack = pack(nearby, real[:, CORE:], imag[:, CORE:])
        put_rows(send_far, layer, far_pack)
        put_rows(send_near, layer, near_pack)
        if layer > 0:
            t_real, t_imag = tile[layer, 0], tile[layer, 1]
            u_real, u_imag = propagate(
                tables,
                t_real * u_real + t_imag * u_imag,
                t_real * u_imag - t_imag * u_real,
                wave,
                -1,
            )


def call(body, outs, scratch=(), smem=0, count=0, limit=8, name=None):
    return pl.pallas_call(
        body,
        out_shape=[jax.ShapeDtypeStruct(shape, jnp.float32) for shape in outs],
        in_specs=[pl.BlockSpec(memory_space=pltpu.SMEM)] * smem
        + [pl.BlockSpec(memory_space=pltpu.VMEM)] * count,
        out_specs=[pl.BlockSpec(memory_space=pltpu.VMEM)] * len(outs),
        scratch_shapes=list(scratch),
        compiler_params=pltpu.CompilerParams(vmem_limit_bytes=limit << 20),
        name=name or body.__name__,
    )


PACK = (SLICES, TILE, CORE)
HALF = (SLICES, CORE, CORE)
RIMS = (2, SLICES, MARGIN, CORE)


def step(blocks, cuts, *args):
    out = call(
        functools.partial(step_kernel, blocks, cuts),
        (PACK, PACK) + ((PACK,) * 2 if cuts == 1 else (HALF,) * 4),
        (
            pltpu.VMEM((SLICES, 2, TILE, TILE), jnp.float32),
            pltpu.VMEM((SLICES - 1, 2, TILE, TILE), jnp.float32),
        ),
        count=4 * blocks + 4,
        limit=24,
        name="step_kernel",
    )(*args)
    return out[:2], out[2 : 2 + cuts], out[2 + cuts :]


def three(value):
    high = value.astype(jnp.bfloat16)
    rest = value - high.astype(jnp.float32)
    middle = rest.astype(jnp.bfloat16)
    low = (rest - middle.astype(jnp.float32)).astype(jnp.bfloat16)
    return high, middle, low


def reorder(order, value):
    high, middle, low = three(value)
    rows = (dot(order[0], high) + dot(order[0], middle)) + dot(order[0], low)
    high, middle, low = three(rows)
    return (dot(high, order[1]) + dot(middle, order[1])) + dot(low, order[1])


def setup_kernel(positions, probe, phase, patterns, order, lit, ordered_phase, ordered_patterns):
    rows = lax.rem(positions[0] + (TILE - MARGIN), TILE)
    cols = lax.rem(positions[1] + (TILE - MARGIN), TILE)
    for part in range(2):
        lit[part] = pltpu.roll(pltpu.roll(probe[part], rows, 0), cols, 1)
    ordered_phase[...] = reorder(order, phase[...])
    ordered_patterns[...] = reorder(order, patterns[...])


def setup(positions, probe, phase, patterns, order):
    shapes = ((2, TILE, TILE), (TILE, TILE), (TILE, TILE))
    return call(setup_kernel, shapes, smem=1, count=4)(positions, probe, phase, patterns, order)


def open_kernel(core, first, second, near, far):
    even = even_row()
    nearby = near_lanes(CORE)
    for layer in range(SLICES):
        packs = pack(nearby, core[layer, 0], core[layer, 1])
        for k, (value, whole) in enumerate(zip(packs, (first, second))):
            whole[layer] = value
            near[k, layer] = jnp.where(even, value[MARGIN:], value[:MARGIN])
            far[k, layer] = jnp.where(even, value[:MARGIN], value[MARGIN:])


def begin(core):
    return call(open_kernel, (HALF, HALF, RIMS, RIMS), count=1)(core)


def assemble_kernel(core_1, core_2, near, far, first, second):
    even = even_row()
    for k, (core, mid) in enumerate(((core_1, first), (core_2, second))):
        for layer in range(SLICES):
            mid[layer, :CORE] = core[layer]
            mid[layer, CORE : CORE + MARGIN] = jnp.where(even, near[k, layer], far[k, layer])
            mid[layer, CORE + MARGIN :] = jnp.where(even, far[k, layer], near[k, layer])


def assemble(*args):
    return call(assemble_kernel, (PACK, PACK), count=4)(*args)


def share_kernel(part_1, part_2, came_1, came_2, total, send_near, send_far):
    even = even_row()
    for k, (part, came) in enumerate(((part_1, came_1), (part_2, came_2))):
        for layer in range(SLICES):
            value = part[layer] + came[layer]
            total[k, layer] = value
            a, b, d, e = (value[n * MARGIN : (n + 1) * MARGIN] for n in range(4))
            send_near[k, layer, :MARGIN] = jnp.where(even, b, e)
            send_near[k, layer, MARGIN:] = jnp.where(even, d, a)
            send_far[k, layer, :MARGIN] = jnp.where(even, e, b)
            send_far[k, layer, MARGIN:] = jnp.where(even, a, d)


def share(*args):
    return call(share_kernel, ((2, *PACK), (2, *HALF), (2, *HALF)), count=4)(*args)


def update_kernel(mid_1, mid_2, total, near, far, new_1, new_2):
    even = even_row()
    row = lax.axis_index("ty")
    above = jnp.where(row == 0, 0.0, STEP_SIZE)
    below = jnp.where(row == lax.axis_size("ty") - 1, 0.0, STEP_SIZE)
    for k, (mid, new) in enumerate(((mid_1, new_1), (mid_2, new_2))):
        for layer in range(SLICES):
            e, o = near[k, layer], far[k, layer]
            down = jnp.where(even, e, o)
            up = jnp.where(even, o, e)
            for n, (added, scale) in enumerate(
                (
                    (up[MARGIN:], STEP_SIZE),
                    (down[:MARGIN], STEP_SIZE),
                    (down[MARGIN:], below),
                    (up[:MARGIN], above),
                )
            ):
                rows = pl.ds(n * MARGIN, MARGIN)
                new[layer, rows] = mid[layer, rows] - scale * (total[k, layer, rows] + added)


def update(*args):
    return call(update_kernel, (PACK, PACK), count=5)(*args)


def close_kernel(part_1, part_2, came_1, came_2, send_near, send_far):
    even = even_row()
    for k, (part, came) in enumerate(((part_1, came_1), (part_2, came_2))):
        for layer in range(SLICES):
            value = part[layer, CORE:] + came[layer]
            below, above = value[:MARGIN], value[MARGIN:]
            send_near[k, layer] = jnp.where(even, below, above)
            send_far[k, layer] = jnp.where(even, above, below)


def close(*args):
    return call(close_kernel, (RIMS, RIMS), count=4)(*args)


def finish_kernel(mid_1, mid_2, part_1, part_2, came_1, came_2, near, far, out):
    even = even_row()
    nearby = near_lanes(MARGIN)
    for layer in range(SLICES):
        for half in range(2):
            rows = pl.ds(half * MARGIN, MARGIN)
            packs = []
            for k, (mid, part, came) in enumerate(
                ((mid_1, part_1, came_1), (mid_2, part_2, came_2))
            ):
                e, o = near[k, layer], far[k, layer]
                added = jnp.where(even, o, e) if half == 0 else jnp.where(even, e, o)
                total = part[layer, rows] + came[layer, rows]
                packs.append(mid[layer, rows] - STEP_SIZE * (total + added))
            out[layer, 0, rows], out[layer, 1, rows] = unpack(nearby, *packs)


def finish(*args):
    return call(finish_kernel, ((SLICES, 2, CORE, CORE),), count=8)(*args)[0]


def swap(axis, first, block):
    count = lax.axis_size(axis)
    pairs = [(i, i + 1) for i in range(first, count - 1, 2)]
    return lax.ppermute(block, axis, pairs + [(j, i) for i, j in pairs])


def swap_rows(near, far):
    far = swap("ty", 1, far)
    return swap("ty", 0, near), far


def swap_cols(near, far):
    far = swap("tx", 1, far)
    near = swap("tx", 0, near)
    return near, far


def shards(object_field, probe, propagator_phase, patterns, scan_positions):
    first, second, near, far = begin(object_field)
    near, far = swap_rows(near, far)
    lit, phase, ordered = setup(
        scan_positions[0, 0, 0], probe, propagator_phase, patterns[0, 0, 0], order_table()
    )
    wave = jnp.stack([jnp.cos(phase), jnp.sin(phase)])
    tables = jnp.asarray(half_tables())
    shared = (lit, wave, ordered, tables)
    first, second = assemble(first, second, near, far)
    near, far = swap_cols(first, second)
    parts, (near,), (far,) = step(1, 1, first, second, near, far, *shared)

    near, far = swap_cols(near, far)
    total, near, far = share(*parts, near, far)
    near, far = swap_rows(near, far)
    first, second = update(first, second, total, near, far)
    near, far = swap_cols(first, second)
    parts, near, far = step(1, 2, first, second, near, far, *shared)

    rim_near, rim_far = swap_cols(near[1], far[1])
    core_near, core_far = swap_cols(near[0], far[0])
    near, far = swap_rows(*close(*parts, rim_near, rim_far))
    return finish(first, second, *parts, core_near, core_far, near, far)


def solution(mesh):
    placed = (
        P(None, None, "ty", "tx"),
        P(),
        P(),
        P("ty", "tx", None, None, None),
        P("ty", "tx", None, None),
    )
    return jax.shard_map(
        shards, mesh=mesh, in_specs=placed, out_specs=P(None, None, "ty", "tx"), check_vma=False
    )
```
